768 devices in a mesh: sample: 24 (over x, z_lo, core), chan: 32 (over z_hi, y).
Axes of the slice: x: 4, y: 8, z: 12 (z_hi: 4, z_lo: 3; z = z_hi * 3 + z_lo), core: 2. Of those that a mesh axis runs over, the one named last changes fastest.
Arguments:
- act_64: bfloat16 [24, 64, 8, 8, 256], P('sample'), may hold values from -6 to 6
- cot_32: bfloat16 [24, 32, 4, 4, 512], P('sample', None, None, None, 'chan'), may hold values from -2.5 to 2.5
- filters_32: bfloat16 [3, 3, 3, 256, 512], P(None, None, None, None, 'chan'), may hold values from -0.078125 to 0.078125
- act_128: bfloat16 [24, 128, 16, 16, 128], P('sample', 'chan'), may hold values from -6 to 6
Outputs:
- grad_filters_32: float32 [3, 3, 3, 256, 512], P(None, None, None, None, 'chan')
- grad_filters_64: float32 [3, 3, 3, 128, 256], P(None, None, None, 'chan')
- cot_64: float32 [24, 64, 8, 8, 256], P('sample', 'chan')
The draws below stay inside these ranges and needn't reach their ends.
All inputs are finite; a program needn't handle non-finite values.
Results may differ from the reference program's by a relative error of at most 0.0029.
Values may be sent and summed in bfloat16 or wider, within the bound.
A program may use at most 64 MiB of HBM per device.

```python
import jax
import jax.numpy as jnp
from jax import lax

C1IN = 128
C2IN = 256
C2OUT = 512
DEPTH = 32
SIDE = 4
SAMPLES = 24
N_CHAN = 32


def raised(drawn, rng, source, target, shards_of, factor):
    def block_of(position):
        return (jnp.arange(drawn.shape[position]) // (drawn.shape[position] // shards_of)).reshape((-1,) + (1,) * (drawn.ndim - 1 - position))

    one_side = jax.random.permutation(rng, shards_of)[block_of(target)]
    far = (block_of(target) + shards_of // 2) % shards_of
    return jnp.where((block_of(source) == one_side) | (block_of(source) == far), factor * drawn, drawn)


def block_scale(rng, shape, cuts, smallest, high):
    def one(dim, blocks):
        heights = jax.random.uniform(jax.random.fold_in(jax.random.fold_in(rng, 6), dim), (blocks,), jnp.float32, smallest / len(cuts), high / len(cuts))
        return jnp.repeat(jnp.exp(heights), shape[dim] // blocks).reshape((-1,) + (1,) * (len(shape) - dim - 1))

    level = one(*cuts[0])
    for cut in cuts[1:]:
        level = level * one(*cut)
    return level


def normal_values(key, dims, width, limit, split=(), held_as=jnp.bfloat16):
    drawn = jax.random.normal(key, dims, jnp.float32) * width
    if len(split) > 0:
        drawn = block_scale(key, dims, split, -0.22, 0.18) * drawn
    return jnp.clip(drawn, min=-limit, max=limit).astype(held_as)


def heavy_noise(rng, dims, deviation, limit, cuts, heavy, held_as=jnp.bfloat16):
    result = deviation * jax.random.normal(rng, dims, jnp.float32)
    if cuts:
        result = result * block_scale(rng, dims, cuts, -0.22, 0.18)
    return jnp.clip(raised(result, jax.random.fold_in(rng, 3), *heavy), -limit, limit).astype(held_as)


def setup_inputs(seed: int = 0) -> dict:
    splits = jax.random.split(jax.random.key(seed), 5)
    return {
        "act_64": normal_values(splits[0], (SAMPLES, 2 * DEPTH, 2 * SIDE, 2 * SIDE, C2IN), 1.0, 6.0, ((0, 24),)),
        "cot_32": heavy_noise(splits[1], (SAMPLES, DEPTH, SIDE, SIDE, C2OUT), 0.2, 2.5, ((0, 24), (4, 32)), (4, 1, 32, 2.75)),
        "filters_32": normal_values(splits[2], (3, 3, 3, C2IN, C2OUT), (27 * C2IN) ** -0.5, 0.078125, ((4, 32),)),
        "act_128": normal_values(splits[3], (SAMPLES, 4 * DEPTH, 4 * SIDE, 4 * SIDE, C1IN), 1.0, 6.0, ((0, 24), (1, 32))),
    }


leak_slope = 0.3

def strided_conv(volume, filters):
    return lax.conv_general_dilated(volume[None], filters, (2, 2, 2), ((1, 1), (1, 1), (1, 1)), dimension_numbers=('NDHWC', 'DHWIO', 'NDHWC'), precision=lax.Precision.HIGHEST)[0]

def valid_conv(volume, filters):
    return lax.conv_general_dilated(volume[None], filters, (2, 2, 2), ((0, 0), (0, 0), (0, 0)), dimension_numbers=('NDHWC', 'DHWIO', 'NDHWC'), precision=lax.Precision.HIGHEST)[0]

def reference(act_64, cot_32, filters_32, act_128):
    filters_full = filters_32.astype(jnp.float32)
    slab_planes = 2 * DEPTH // N_CHAN
    lower_in = act_128.shape[4]
    lower_out = act_64.shape[4]

    def one_volume(carry, inputs):
        volume_64, cot_single, volume_128 = inputs
        volume_upper = volume_64.astype(jnp.float32)
        unused_out, pull_back = jax.vjp(strided_conv, volume_upper, filters_full)
        grad_volume, grad_filters = pull_back(cot_single.astype(jnp.float32))
        cot_lower = (grad_volume * jnp.where(volume_upper > 0, 1.0, leak_slope)).astype(jnp.float32)
        cot_float = cot_lower.astype(jnp.bfloat16).astype(jnp.float32)
        padded_lower = jnp.pad(volume_128.astype(jnp.float32), ((1, 1), (1, 1), (1, 1), (0, 0)))

        def one_slab(total, block):
            window = lax.dynamic_slice_in_dim(padded_lower, block * (2 * slab_planes), 2 * slab_planes + 1, 0)
            cot_slab = lax.dynamic_slice_in_dim(cot_float, block * slab_planes, slab_planes, 0)
            zero_filters = jnp.zeros((3, 3, 3, lower_in, lower_out), jnp.float32)
            unused_slab, pull_slab = jax.vjp(lambda weights: valid_conv(window, weights), zero_filters)
            term = pull_slab(cot_slab)[0]
            return (total + term, None)
        blocks = jnp.arange(N_CHAN, dtype=jnp.int32)
        grad_lower, unused_blocks = lax.scan(one_slab, jnp.zeros((3, 3, 3, lower_in, lower_out), jnp.float32), blocks)
        return ((carry[0] + grad_filters, carry[1] + grad_lower), cot_lower)
    start_carry = (jnp.zeros(filters_32.shape, jnp.float32), jnp.zeros((3, 3, 3, lower_in, lower_out), jnp.float32))
    totals, cot_all = lax.scan(one_volume, start_carry, (act_64, cot_32, act_128))
    return (totals[0] / SAMPLES, totals[1] / SAMPLES, cot_all)
```

```python
import jax
import jax.numpy as jnp
import numpy as np
from jax import lax
from jax.experimental import pallas as pl
from jax.experimental.pallas import tpu as pltpu
from jax.sharding import PartitionSpec as P

leak_slope = 0.3
BF = jnp.bfloat16
F32 = jnp.float32
NX, NZL, NC = 4, 3, 2
NZH, NY = 4, 8
NM = NX * NC
NZ = NZH * NZL
PIECE = 56


def tap_of(par, shift):
    if par == 0:
        return 1 if shift == 0 else None
    return 2 if shift == 0 else 0


def class_taps(p):
    found = []
    for q in range(8):
        taps = [tap_of((p >> b) & 1, (q >> b) & 1) for b in (2, 1, 0)]
        if None not in taps:
            found.append((q, taps[0] * 9 + taps[1] * 3 + taps[2]))
    return found


def tables():
    split = np.zeros((256, 256), np.float32)
    for p in range(8):
        pz, py, px = p >> 2, (p >> 1) & 1, p & 1
        for a in range(2):
            for b in range(4):
                for c in range(4):
                    split[p * 32 + a * 16 + b * 4 + c, (2 * a + pz) * 64 + (2 * b + py) * 8 + 2 * c + px] = 1
    merge = np.zeros((128, 128), np.float32)
    for p in range(8):
        pz, py, px = p >> 2, (p >> 1) & 1, p & 1
        for b in range(4):
            for c in range(4):
                merge[pz * 64 + (2 * b + py) * 8 + 2 * c + px, p * 16 + b * 4 + c] = 1
    spread16 = np.zeros((16, 128), np.float32)
    for q in range(8):
        for f in range(16):
            spread16[f, q * 16 + f] = 1
    shift = np.zeros((128, 512), np.float32)
    for k in range(4):
        dy, dx = k >> 1, k & 1
        for a in range(8):
            for b in range(4 - dy):
                for c in range(4 - dx):
                    shift[a * 16 + b * 4 + c, k * 128 + a * 16 + (b + dy) * 4 + c + dx] = 1
    order = np.zeros((128, 128), np.float32)
    for m in range(NM):
        for h in range(2):
            for y in range(8):
                order[m * 16 + h * 8 + y, 4 * ((2 * (m % 2) + h) * 8 + y) + m // 2] = 1
    pick = np.zeros((9, 512, 128), np.float32)
    for j in range(3):
        for k in range(3):
            for z in range(2):
                for y in range(8):
                    for x in range(8):
                        row, col = 2 * y + j - 1, 2 * x + k - 1
                        if row >= 0 and col >= 0:
                            pick[j * 3 + k, z * 256 + row * 16 + col, z * 64 + y * 8 + x] = 1
    return split, merge, spread16, shift, order, pick


def mm(a, b):
    return jnp.dot(a, b, preferred_element_type=F32)


def kernel(
    act_ref, cot_ref, filt_ref, low_ref,
    split_ref, merge_ref, spread_ref, shift_ref, order_ref, pick_ref,
    out_up, out_low, out_cot,
    w_ref, wq_ref, a_ref, u_ref, urecv, uzl, ufin,
    fm1, fp1, fp2, r_ref, part, rplus, rminus,
    rim, t_ref, lstack, lsend, lrecv, cown, crecv, res,
    dsend, drecv, ssum, zsend, zrecv, xrecv,
    send_sem, recv_sem,
):
    s = lax.axis_index("sample")
    ch = lax.axis_index("chan")
    c = s % 2
    zl = (s // 2) % 3
    x = s // 6
    y = ch % 8
    zh = ch // 8
    m = x * 2 + c

    def at_zh(d):
        return (s, lax.rem(zh + d, NZH) * 8 + y)

    def at_y(d):
        return (s, zh * 8 + lax.rem(y + d, NY))

    def m_at(r):
        return lax.rem(m + r, NM)

    def at_m(r):
        mm_ = m_at(r)
        return (((mm_ // 2) * 3 + zl) * 2 + mm_ % 2, ch)

    def at_z(zl_, zh_):
        return ((x * 3 + zl_) * 2 + c, zh_ * 8 + y)

    counter = [0]
    pending = []

    def remote(src, dst, dev):
        i = counter[0]
        counter[0] += 1
        cp = pltpu.make_async_remote_copy(
            src_ref=src, dst_ref=dst, send_sem=send_sem.at[i], recv_sem=recv_sem.at[i],
            device_id=dev, device_id_type=pl.DeviceIdType.MESH,
        )
        cp.start()
        pending.append(cp)
        return cp

    barrier = pltpu.get_barrier_semaphore()
    partners = [at_y(d) for d in range(1, 8)] + [at_m(r) for r in range(1, 8)]
    partners += [(s, lax.rem(ch + 1, 32)), (s, lax.rem(ch + 31, 32))]
    for dzl in range(3):
        for dzh in range(4):
            if dzl or dzh:
                partners.append(at_z(lax.rem(zl + dzl, 3), lax.rem(zh + dzh, 4)))
    for dev in partners:
        pl.semaphore_signal(barrier, inc=1, device_id=dev, device_id_type=pl.DeviceIdType.MESH)
    pl.semaphore_wait(barrier, len(partners))

    h0 = 13 * c
    lo, hi = pl.ds(h0, 7), pl.ds(h0 + 7, 7)
    f_p_lo = remote(filt_ref.at[lo], fm1.at[lo], at_zh(1))
    f_m_hi = remote(filt_ref.at[hi], fp1.at[hi], at_zh(3))
    f_p_hi = remote(filt_ref.at[hi], fm1.at[hi], at_zh(1))
    f_m_lo = remote(filt_ref.at[lo], fp1.at[lo], at_zh(3))
    rim_cp = remote(low_ref.at[3], rim, (s, lax.rem(ch + 1, 32)))

    wide = mm(cot_ref[...], spread_ref[...])
    lane = lax.broadcasted_iota(jnp.int32, (128, 128), 1) // 16
    for g in range(4):
        near = wide[128 * g : 128 * g + 128]
        far = wide[128 * g + 16 : 128 * g + 144]
        both = jnp.where(lane >= 4, far, near)
        terms = [jnp.where(lane % 4 == k, both, 0.0).astype(BF) for k in range(4)]
        w_ref[g] = mm(shift_ref[...], jnp.concatenate(terms, axis=0)).astype(BF)
    w_cps = []
    for d in range(1, 4):
        w_cps.append(remote(w_ref.at[lax.rem(zh + d, NZH)], wq_ref.at[4 - d], at_zh(d)))

    def split_group(g, carry):
        got = mm(split_ref[...], act_ref[pl.ds(pl.multiple_of(g * 256, 256), 256), :]).astype(BF)
        for p in range(8):
            a_ref[p, pl.ds(pl.multiple_of(g * 32, 32), 32), :] = got[p * 32 : p * 32 + 32]
        return carry

    lax.fori_loop(0, 16, split_group, 0)

    f_p_lo.wait_recv()
    f2_p = remote(fm1.at[lo], fp2.at[lo], at_zh(1))
    f_m_hi.wait_recv()
    f2_m = remote(fp1.at[hi], fp2.at[hi], at_zh(3))

    wt = jnp.concatenate([jnp.transpose(w_ref[g].astype(F32)) for g in range(4)], axis=1).astype(BF)
    for p in range(8):
        got = mm(wt, a_ref[p])
        for q, tap in class_taps(p):
            u_ref[tap * 16 : tap * 16 + 16, :] = got[q * 16 : q * 16 + 16]
    u_ref[432:448, :] = jnp.zeros((16, 256), F32)
    u_cps = []
    for r in range(1, NM):
        u_cps.append(remote(u_ref.at[pl.ds(m_at(r) * PIECE, PIECE)], urecv.at[r - 1], at_m(r)))

    mate = (s + 1 - 2 * c, ch)
    own_half = pl.ds(14 * c, 13)
    f_p_hi.wait_recv()
    ex1 = remote(fm1.at[own_half], fm1.at[own_half], mate)
    f_m_lo.wait_recv()
    ex2 = remote(fp1.at[own_half], fp1.at[own_half], mate)

    rim_cp.wait_recv()
    edge = rim[...]
    edge = jnp.where(ch == 0, jnp.zeros_like(edge), edge)
    for q in range(5):
        plane = edge if q == 0 else low_ref[q - 1]
        got = lax.dot_general(order_ref[...], plane, (((1,), (1,)), ((), ())), preferred_element_type=F32)
        t_ref[q] = got.astype(BF)
    for i in range(3):
        lstack[i * 128 : i * 128 + 128, 0:256] = t_ref[i]
        lstack[i * 128 : i * 128 + 128, 256:512] = t_ref[i + 2]

    def window(jk, carry):
        got = mm(lstack[...], pick_ref[jk]).astype(BF)
        for i in range(3):
            for k in range(NM):
                lsend[k, i * 9 + jk] = got[i * 128 + k * 16 : i * 128 + k * 16 + 16]
        return carry

    lax.fori_loop(0, 9, window, 0)
    l_cps = []
    for r in range(1, NM):
        l_cps.append(remote(lsend.at[m_at(r)], lrecv.at[r - 1], at_m(r)))

    f2_p.wait_recv()
    f2_m.wait_recv()
    ex3 = remote(fp2.at[own_half], fp2.at[own_half], mate)
    for cp in w_cps:
        cp.wait_recv()
    wq_ref[0] = w_ref[zh]
    for cp in (ex1, ex2, ex3):
        cp.wait_recv()

    shards = (filt_ref, fp1, fp2, fm1)
    left = jnp.concatenate([wq_ref[r] for r in range(4)], axis=1)
    for p in range(8):
        taps = dict(class_taps(p))
        for r in range(4):
            for q in range(8):
                row = r * 128 + q * 16
                if q in taps:
                    r_ref[row : row + 16, :] = shards[r][taps[q]]
                else:
                    r_ref[row : row + 16, :] = jnp.zeros((16, 256), BF)
        got = mm(left, r_ref[...])
        for k in range(8):
            part[k, p] = got[k * 16 : k * 16 + 16]

    halves = (pl.ds(0, 4), pl.ds(4, 4))
    plus = [[None] * 2 for _ in range(4)]
    minus = [[None] * 2 for _ in range(3)]
    for t in range(4):
        for h in range(2):
            o = lax.rem(y + 4 - t, NY)
            if t:
                plus[t - 1][h].wait_recv()
                part[o, halves[h]] = part[o, halves[h]] + rplus[t - 1, halves[h]]
            plus[t][h] = remote(part.at[o, halves[h]], rplus.at[t, halves[h]], at_y(1))
            if t < 3:
                o = lax.rem(y + 5 + t, NY)
                if t:
                    minus[t - 1][h].wait_recv()
                    part[o, halves[h]] = part[o, halves[h]] + rminus[t - 1, halves[h]]
                minus[t][h] = remote(part.at[o, halves[h]], rminus.at[t, halves[h]], at_y(7))
        if t == 1:
            piece = u_ref[pl.ds(pl.multiple_of(m * PIECE, 8), PIECE), :]
            for r in range(1, NM):
                u_cps[r - 1].wait_recv()
                piece = piece + urecv[r - 1]
            uzl[zl] = piece
            uz_cps = []
            for d in (1, 2):
                uz_cps.append(remote(uzl.at[zl], uzl.at[zl], at_z(lax.rem(zl + d, 3), zh)))
        if t == 3:
            for cp in uz_cps:
                cp.wait_recv()
            ufin[m] = (uzl[0] + uzl[1] + uzl[2]) * (1.0 / 24.0)
    for h in range(2):
        minus[2][h].wait_recv()
        plus[3][h].wait_recv()
    total = part[y] + rplus[3] + rminus[2]
    total = total.reshape(128, 256)
    natural = jnp.dot(merge_ref[...], total, preferred_element_type=F32, precision=lax.Precision.HIGHEST)
    own = act_ref[pl.ds(pl.multiple_of(ch * 128, 128), 128), :].astype(F32)
    cot = natural * jnp.where(own > 0, 1.0, leak_slope)
    out_cot[...] = cot
    cown[...] = cot.astype(BF)
    c_cps = []
    for r in range(1, NM):
        c_cps.append(remote(cown, crecv.at[r - 1], at_m(r)))
    ug_cps = []
    for r in range(1, NM):
        ug_cps.append(remote(ufin.at[m], ufin.at[m], at_m(r)))

    acc = mm(lsend[m].reshape(432, 128), cown[...])
    for r in range(1, NM):
        l_cps[r - 1].wait_recv()
        c_cps[r - 1].wait_recv()
        acc = acc + mm(lrecv[r - 1].reshape(432, 128), crecv[r - 1])
    for half in range(2):
        res[half] = acc[:, 128 * half : 128 * half + 128]
    for k in range(NY):
        for half in range(2):
            got = res[half, pl.ds(k, 54, stride=8), :].astype(BF)
            got = jnp.concatenate([got, jnp.zeros((10, 128), BF)], axis=0)
            dsend[k, :, 128 * half : 128 * half + 128] = got
    d_cps = []
    for r in range(1, NY):
        d_cps.append(remote(dsend.at[lax.rem(y + r, NY)], drecv.at[r - 1], at_y(r)))
    total = [res[half, pl.ds(y, 54, stride=8), :] for half in range(2)]
    for r in range(1, NY):
        d_cps[r - 1].wait_recv()
        for half in range(2):
            total[half] = total[half] + drecv[r - 1, 0:54, 128 * half : 128 * half + 128].astype(F32)
    for half in range(2):
        ssum[half] = total[half]
    for h in range(2):
        for half in range(2):
            got = ssum[half, pl.ds(h, 27, stride=2), :]
            zsend[h, :, 128 * half : 128 * half + 128] = jnp.concatenate([got, jnp.zeros((5, 128), F32)], axis=0)

    myz = zh * 3 + zl
    base = counter[0]
    counter[0] += NZ
    sends = []
    for h in range(2):
        for l in range(3):
            tz = 2 * c + h
            i = counter[0]
            counter[0] += 1
            away = jnp.logical_or(tz != zh, zl != l)
            cp = pltpu.make_async_remote_copy(
                src_ref=zsend.at[h], dst_ref=zrecv.at[myz], send_sem=send_sem.at[i],
                recv_sem=recv_sem.at[base + myz], device_id=at_z(l, tz),
                device_id_type=pl.DeviceIdType.MESH,
            )
            pl.when(away)(cp.start)
            sends.append((away, cp))
    home = zh // 2 == c

    @pl.when(home)
    def _():
        zrecv[myz] = zsend[zh - 2 * c]

    for j in range(NZ):
        cp = pltpu.make_async_remote_copy(
            src_ref=zsend.at[0], dst_ref=zrecv.at[j], send_sem=send_sem.at[base + j],
            recv_sem=recv_sem.at[base + j], device_id=at_z(zl, zh),
            device_id_type=pl.DeviceIdType.MESH,
        )
        pl.when(jnp.logical_and(home, myz != j))(cp.wait_recv)

    base = counter[0]
    counter[0] += NX
    bsends = []

    @pl.when(home)
    def _():
        done = zrecv[0]
        for j in range(1, NZ):
            done = done + zrecv[j]
        xrecv[x] = done * (1.0 / 24.0)

    for r in range(1, NM):
        i = counter[0]
        counter[0] += 1
        cp = pltpu.make_async_remote_copy(
            src_ref=xrecv.at[x], dst_ref=xrecv.at[x], send_sem=send_sem.at[i],
            recv_sem=recv_sem.at[base + x], device_id=at_m(r),
            device_id_type=pl.DeviceIdType.MESH,
        )
        pl.when(home)(cp.start)
        bsends.append(cp)
    for cp in ug_cps:
        cp.wait_recv()
    for k in range(NM):
        out_up[k * PIECE : k * PIECE + PIECE, :] = ufin[k]
    for k in range(NX):
        cp = pltpu.make_async_remote_copy(
            src_ref=xrecv.at[k], dst_ref=xrecv.at[k], send_sem=send_sem.at[base + k],
            recv_sem=recv_sem.at[base + k], device_id=at_m(1),
            device_id_type=pl.DeviceIdType.MESH,
        )
        pl.when(jnp.logical_not(jnp.logical_and(home, x == k)))(cp.wait_recv)
    for k in range(NX):
        out_low[:, k, :] = xrecv[k, 0:27]

    for cp in pending:
        cp.wait_send()
    for away, cp in sends:
        pl.when(away)(cp.wait_send)
    for cp in bsends:
        pl.when(home)(cp.wait_send)


def body(act_64, cot_32, filters_32, act_128):
    consts = [jnp.asarray(t, BF) for t in tables()]
    consts[1] = consts[1].astype(F32)
    act = act_64.reshape(64 * 64, 256)
    cot = jnp.pad(cot_32[0].reshape(512, 16), ((0, 16), (0, 0)))
    filt = filters_32.transpose(0, 1, 2, 4, 3).reshape(27, 16, 256)
    low = act_128.reshape(4, 256, 128)
    vm = pltpu.VMEM
    up, lowg, cot_full = pl.pallas_call(
        kernel,
        out_shape=(
            jax.ShapeDtypeStruct((448, 256), F32),
            jax.ShapeDtypeStruct((27, 4, 256), F32),
            jax.ShapeDtypeStruct((128, 256), F32),
        ),
        in_specs=[pl.BlockSpec(memory_space=pltpu.VMEM)] * 10,
        out_specs=[pl.BlockSpec(memory_space=pltpu.VMEM)] * 3,
        scratch_shapes=[
            vm((4, 128, 128), BF), vm((4, 128, 128), BF), vm((8, 512, 256), BF),
            vm((448, 256), F32), vm((7, PIECE, 256), F32), vm((3, PIECE, 256), F32), vm((NM, PIECE, 256), F32),
            vm((27, 16, 256), BF), vm((27, 16, 256), BF), vm((27, 16, 256), BF),
            vm((512, 256), BF), vm((8, 8, 16, 256), F32), vm((4, 8, 16, 256), F32), vm((3, 8, 16, 256), F32),
            vm((256, 128), BF), vm((5, 128, 256), BF), vm((384, 512), BF),
            vm((NM, 27, 16, 128), BF), vm((7, 27, 16, 128), BF),
            vm((128, 256), BF), vm((7, 128, 256), BF), vm((2, 432, 128), F32),
            vm((8, 64, 256), BF), vm((7, 64, 256), BF), vm((2, 54, 128), F32),
            vm((2, 32, 256), F32), vm((NZ, 32, 256), F32), vm((NX, 32, 256), F32),
            pltpu.SemaphoreType.DMA((112,)), pltpu.SemaphoreType.DMA((112,)),
        ],
        compiler_params=pltpu.CompilerParams(
            collective_id=0, has_side_effects=True, vmem_limit_bytes=48 * 1024 * 1024
        ),
    )(act, cot, filt, low, *consts)
    up = up[:432].reshape(3, 3, 3, 16, 256).transpose(0, 1, 2, 4, 3)
    return up, lowg.reshape(3, 3, 3, 4, 256), cot_full.reshape(1, 2, 8, 8, 256)


def solution(mesh):
    placed = (
        P("sample", None, None, None, None),
        P("sample", None, None, None, "chan"),
        P(None, None, None, None, "chan"),
        P("sample", "chan", None, None, None),
    )
    return jax.shard_map(
        body,
        mesh=mesh,
        in_specs=placed,
        out_specs=(
            P(None, None, None, None, "chan"),
            P(None, None, None, "chan", None),
            P("sample", "chan", None, None, None),
        ),
        check_vma=False,
    )
```

```python
import jax
import jax.numpy as jnp
import numpy as np
from jax import lax
from jax.experimental import pallas as pl
from jax.experimental.pallas import tpu as pltpu
from jax.sharding import PartitionSpec as P

leak_slope = 0.3
BF = jnp.bfloat16
F32 = jnp.float32
NX, NZL, NC = 4, 3, 2
NZH, NY = 4, 8
NM = NX * NC
NZ = NZH * NZL
PIECE = 56


def tap_of(par, shift):
    if par == 0:
        return 1 if shift == 0 else None
    return 2 if shift == 0 else 0


def class_taps(p):
    found = []
    for q in range(8):
        taps = [tap_of((p >> b) & 1, (q >> b) & 1) for b in (2, 1, 0)]
        if None not in taps:
            found.append((q, taps[0] * 9 + taps[1] * 3 + taps[2]))
    return found


def tables():
    split = np.zeros((256, 256), np.float32)
    for p in range(8):
        pz, py, px = p >> 2, (p >> 1) & 1, p & 1
        for a in range(2):
            for b in range(4):
                for c in range(4):
                    split[p * 32 + a * 16 + b * 4 + c, (2 * a + pz) * 64 + (2 * b + py) * 8 + 2 * c + px] = 1
    merge = np.zeros((128, 128), np.float32)
    for p in range(8):
        pz, py, px = p >> 2, (p >> 1) & 1, p & 1
        for b in range(4):
            for c in range(4):
                merge[pz * 64 + (2 * b + py) * 8 + 2 * c + px, p * 16 + b * 4 + c] = 1
    spread16 = np.zeros((16, 128), np.float32)
    for q in range(8):
        for f in range(16):
            spread16[f, q * 16 + f] = 1
    shift = np.zeros((128, 512), np.float32)
    for k in range(4):
        dy, dx = k >> 1, k & 1
        for a in range(8):
            for b in range(4 - dy):
                for c in range(4 - dx):
                    shift[a * 16 + b * 4 + c, k * 128 + a * 16 + (b + dy) * 4 + c + dx] = 1
    order = np.zeros((128, 128), np.float32)
    for m in range(NM):
        for h in range(2):
            for y in range(8):
                order[m * 16 + h * 8 + y, 4 * ((2 * (m % 2) + h) * 8 + y) + m // 2] = 1
    pick = np.zeros((9, 512, 128), np.float32)
    for j in range(3):
        for k in range(3):
            for z in range(2):
                for y in range(8):
                    for x in range(8):
                        row, col = 2 * y + j - 1, 2 * x + k - 1
                        if row >= 0 and col >= 0:
                            pick[j * 3 + k, z * 256 + row * 16 + col, z * 64 + y * 8 + x] = 1
    return split, merge, spread16, shift, order, pick


def mm(a, b):
    return jnp.dot(a, b, preferred_element_type=F32)


def kernel(
    act_hbm, cot_hbm, filt_hbm, low_hbm,
    split_hbm, merge_hbm, spread_hbm, shift_hbm, order_hbm, pick_hbm,
    out_up, out_low, out_cot,
    act_ref, cot_ref, fbuf, low_ref,
    split_ref, merge_ref, spread_ref, shift_ref, order_ref, pick_ref,
    wide_ref, w_ref, wq_ref, a_ref, u_ref, urecv, uzl, ufin,
    r_ref, part, rlong, rshort,
    rim, t_ref, lstack, lsend, lrecv, call, res,
    dsend, drecv, ssum, zsend, zrecv, xrecv,
    load_sem, send_sem, recv_sem,
):
    s = lax.axis_index("sample")
    ch = lax.axis_index("chan")
    c = s % 2
    zl = (s // 2) % 3
    x = s // 6
    y = ch % 8
    zh = ch // 8
    m = x * 2 + c
    mate = (s + 1 - 2 * c, ch)

    def at_zh(d):
        return (s, lax.rem(zh + d, NZH) * 8 + y)

    def at_y(d):
        return (s, zh * 8 + lax.rem(y + d, NY))

    def m_at(r):
        return lax.rem(m + r, NM)

    def at_m(r):
        other = m_at(r)
        return (((other // 2) * 3 + zl) * 2 + other % 2, ch)

    def at_x(r):
        return ((lax.rem(x + r, NX) * 3 + zl) * 2 + c, ch)

    def from_x(r, core):
        return lax.rem(x + NX - r, NX) * 2 + core

    def at_z(zl_, zh_):
        return ((x * 3 + zl_) * 2 + c, zh_ * 8 + y)

    counter = [0]
    pending = []

    def remote(src, dst, dev):
        i = counter[0]
        counter[0] += 1
        cp = pltpu.make_async_remote_copy(
            src_ref=src, dst_ref=dst, send_sem=send_sem.at[i], recv_sem=recv_sem.at[i],
            device_id=dev, device_id_type=pl.DeviceIdType.MESH,
        )
        cp.start()
        pending.append(cp)
        return cp

    barrier = pltpu.get_barrier_semaphore()
    partners = [at_y(d) for d in range(1, 8)] + [at_m(r) for r in range(1, 8)]
    partners += [(s, lax.rem(ch + 1, 32)), (s, lax.rem(ch + 31, 32))]
    for dzl in range(3):
        for dzh in range(4):
            if dzl or dzh:
                partners.append(at_z(lax.rem(zl + dzl, 3), lax.rem(zh + dzh, 4)))
    for dev in partners:
        pl.semaphore_signal(barrier, inc=1, device_id=dev, device_id_type=pl.DeviceIdType.MESH)

    loads = {}
    for i, (name, src, dst) in enumerate((
        ("cot", cot_hbm, cot_ref), ("spread", spread_hbm, spread_ref), ("shift", shift_hbm, shift_ref),
        ("f0", filt_hbm.at[:, :, 0:128], fbuf.at[0, 0, 0:27]), ("f1", filt_hbm.at[:, :, 128:256], fbuf.at[0, 1, 0:27]),
        ("low", low_hbm, low_ref), ("split", split_hbm, split_ref), ("act", act_hbm, act_ref),
        ("order", order_hbm, order_ref), ("pick", pick_hbm, pick_ref), ("merge", merge_hbm, merge_ref),
    )):
        cp = pltpu.make_async_copy(src, dst, load_sem.at[i])
        cp.start()
        loads[name] = cp
    fbuf[0, :, 27] = jnp.zeros((2, 16, 128), BF)

    for name in ("cot", "spread", "shift"):
        loads[name].wait()
    for bc in range(16):
        got = lax.dot_general(
            cot_ref[bc * 16 : bc * 16 + 16, :], spread_ref[...], (((0,), (0,)), ((), ())), preferred_element_type=F32
        )
        wide_ref[pl.ds(bc, 32, stride=16), :] = got
    wide_ref[512:528, :] = jnp.zeros((16, 128), F32)
    lane = lax.broadcasted_iota(jnp.int32, (128, 128), 1) // 16
    for g in range(4):
        near = wide_ref[128 * g : 128 * g + 128, :]
        far = wide_ref[128 * g + 16 : 128 * g + 144, :]
        both = jnp.where(lane >= 4, far, near)
        terms = [jnp.where(lane % 4 == k, both, 0.0).astype(BF) for k in range(4)]
        w_ref[g] = mm(shift_ref[...], jnp.concatenate(terms, axis=0)).astype(BF)
    for name in ("f0", "f1", "low"):
        loads[name].wait()

    pl.semaphore_wait(barrier, len(partners))

    share = pl.ds(7 * x, 7)
    f_z = {}
    for d in (2, 1, 3):
        f_z[d] = remote(fbuf.at[0, c, share], fbuf.at[4 - d, c, share], at_zh(d))
    rim_cp = remote(low_ref.at[3], rim, (s, lax.rem(ch + 1, 32)))
    w_cps = []
    for d in (2, 1, 3):
        w_cps.append(remote(w_ref.at[lax.rem(zh + d, NZH)], wq_ref.at[4 - d], at_zh(d)))

    loads["split"].wait()
    loads["act"].wait()

    def split_group(g, carry):
        got = mm(split_ref[...], act_ref[pl.ds(pl.multiple_of(g * 256, 256), 256), :]).astype(BF)
        for p in range(8):
            a_ref[p, pl.ds(pl.multiple_of(g * 32, 32), 32), :] = got[p * 32 : p * 32 + 32]
        return carry

    lax.fori_loop(0, 16, split_group, 0)

    f_x = {}
    f_c = {}

    def spread_x(d):
        f_z[d].wait_recv()
        f_x[d] = [remote(fbuf.at[4 - d, c, share], fbuf.at[4 - d, c, share], at_x(r)) for r in (2, 1, 3)]

    def spread_c(d):
        for cp in f_x[d]:
            cp.wait_recv()
        f_c[d] = remote(fbuf.at[4 - d, c], fbuf.at[4 - d, c], mate)

    spread_x(1)
    spread_x(3)

    wt = jnp.concatenate([jnp.transpose(w_ref[g].astype(F32)) for g in range(4)], axis=1).astype(BF)
    for p in range(8):
        got = mm(wt, a_ref[p])
        for q, tap in class_taps(p):
            u_ref[tap * 16 : tap * 16 + 16, :] = got[q * 16 : q * 16 + 16]
    u_ref[432:448, :] = jnp.zeros((16, 256), F32)
    spread_x(2)
    spread_c(1)
    spread_c(3)
    u_cps = []
    for r in range(1, NM):
        u_cps.append(remote(u_ref.at[pl.ds(m_at(r) * PIECE, PIECE)], urecv.at[r - 1], at_m(r)))

    loads["order"].wait()
    loads["pick"].wait()
    rim_cp.wait_recv()
    edge = rim[...]
    edge = jnp.where(ch == 0, jnp.zeros_like(edge), edge)
    for q in range(5):
        plane = edge if q == 0 else low_ref[q - 1]
        got = lax.dot_general(order_ref[...], plane, (((1,), (1,)), ((), ())), preferred_element_type=F32)
        t_ref[q] = got.astype(BF)
    for i in range(3):
        lstack[i * 128 : i * 128 + 128, 0:256] = t_ref[i]
        lstack[i * 128 : i * 128 + 128, 256:512] = t_ref[i + 2]
    spread_c(2)

    for cp in w_cps:
        cp.wait_recv()
    wq_ref[0] = w_ref[zh]
    left = jnp.concatenate([wq_ref[r] for r in range(4)], axis=1)
    for d in (1, 3, 2):
        f_c[d].wait_recv()

    def partial(p):
        taps = dict(class_taps(p))
        for r in range(4):
            for q in range(8):
                row = r * 128 + q * 16
                for half in range(2):
                    lanes = slice(128 * half, 128 * half + 128)
                    if q in taps:
                        r_ref[p % 2, row : row + 16, lanes] = fbuf[r, half, taps[q]]
                    else:
                        r_ref[p % 2, row : row + 16, lanes] = jnp.zeros((16, 128), BF)
        got = mm(left, r_ref[p % 2])
        for k in range(8):
            part[k, p] = got[k * 16 : k * 16 + 16]

    halves = (pl.ds(0, 4), pl.ds(4, 4))
    way = (1, 7)
    back = (7, 1)
    longs = [[None] * 2 for _ in range(4)]
    shorts = [[None] * 2 for _ in range(3)]

    def ring(t, h):
        o = lax.rem(y + way[h] * (4 - t), NY)
        if t:
            longs[t - 1][h].wait_recv()
            part[o, halves[h]] = part[o, halves[h]] + rlong[t - 1, halves[h]]
        longs[t][h] = remote(part.at[o, halves[h]], rlong.at[t, halves[h]], at_y(way[h]))
        if t < 3:
            o = lax.rem(y + back[h] * (3 - t), NY)
            if t:
                shorts[t - 1][h].wait_recv()
                part[o, halves[h]] = part[o, halves[h]] + rshort[t - 1, halves[h]]
            shorts[t][h] = remote(part.at[o, halves[h]], rshort.at[t, halves[h]], at_y(back[h]))

    for p in range(4):
        partial(p)
    ring(0, 0)
    for p in range(4, 8):
        partial(p)
    ring(0, 1)

    def window(jk, carry):
        got = mm(lstack[...], pick_ref[jk]).astype(BF)
        for i in range(3):
            for k in range(NM):
                lsend[k, i * 9 + jk] = got[i * 128 + k * 16 : i * 128 + k * 16 + 16]
        return carry

    lax.fori_loop(0, 3, window, 0)
    ring(1, 0)
    ring(1, 1)
    lax.fori_loop(3, 9, window, 0)
    l_cps = []
    for r in range(1, NM):
        l_cps.append(remote(lsend.at[m_at(r)], lrecv.at[m], at_m(r)))
    ring(2, 0)
    ring(2, 1)
    piece = u_ref[pl.ds(pl.multiple_of(m * PIECE, 8), PIECE), :]
    for r in range(1, NM):
        u_cps[r - 1].wait_recv()
        piece = piece + urecv[r - 1]
    uzl[zl] = piece
    uz_cps = []
    for d in (1, 2):
        uz_cps.append(remote(uzl.at[zl], uzl.at[zl], at_z(lax.rem(zl + d, 3), zh)))
    ring(3, 0)
    ring(3, 1)

    loads["merge"].wait()
    c_x = [[None] * 4 for _ in range(2)]
    c_m = [None] * 2
    for h in range(2):
        shorts[2][h].wait_recv()
        longs[3][h].wait_recv()
        total = part[y, halves[h]] + rlong[3, halves[h]] + rshort[2, halves[h]]
        total = total.reshape(64, 256)
        natural = jnp.dot(merge_ref[...], total, preferred_element_type=F32, precision=lax.Precision.HIGHEST)
        own = act_ref[pl.ds(pl.multiple_of(ch * 128 + h * 64, 64), 64), :].astype(F32)
        cot = natural * jnp.where(own > 0, 1.0, leak_slope)
        out_cot[h * 64 : h * 64 + 64, :] = cot
        call[m, h] = cot.astype(BF)
        for r in (2, 1, 3):
            c_x[h][r] = remote(call.at[m, h], call.at[m, h], at_x(r))
        c_m[h] = remote(call.at[m, h], call.at[m, h], mate)

    def term(lhs, src):
        rhs = jnp.concatenate([call[src, 0], call[src, 1]], axis=0)
        return mm(lhs.reshape(432, 128), rhs)

    acc = term(lsend[m], m)
    for cp in l_cps:
        cp.wait_recv()
    c_f = [[None] * 4 for _ in range(2)]
    for h in range(2):
        for r in (1, 3, 2):
            c_x[h][r].wait_recv()
            got = from_x(r, c)
            c_f[h][r] = remote(call.at[got, h], call.at[got, h], mate)
    for h in range(2):
        c_m[h].wait_recv()
    acc = acc + term(lrecv[x * 2 + 1 - c], x * 2 + 1 - c)
    for r in (1, 3, 2):
        acc = acc + term(lrecv[from_x(r, c)], from_x(r, c))
    for cp in uz_cps:
        cp.wait_recv()
    ufin[m] = (uzl[0] + uzl[1] + uzl[2]) * (1.0 / 24.0)
    for r in (1, 3, 2):
        for h in range(2):
            c_f[h][r].wait_recv()
        acc = acc + term(lrecv[from_x(r, 1 - c)], from_x(r, 1 - c))
    for half in range(2):
        res[half] = acc[:, 128 * half : 128 * half + 128]

    d_cps = [[None] * NY for _ in range(2)]
    for half in range(2):
        for k in range(NY):
            got = res[half, pl.ds(k, 54, stride=8), :].astype(BF)
            dsend[half, k] = jnp.concatenate([got, jnp.zeros((10, 128), BF)], axis=0)
        for r in (4, 3, 5, 2, 6, 1, 7):
            d_cps[half][r] = remote(dsend.at[half, lax.rem(y + r, NY)], drecv.at[half, r - 1], at_y(r))
    ug_cps = []
    for r in range(1, NM):
        ug_cps.append(remote(ufin.at[m], ufin.at[m], at_m(r)))

    myz = zh * 3 + zl
    home = zh // 2 == c
    zbase = counter[0]
    counter[0] += 2 * NZ
    zsends = []
    for half in range(2):
        total = res[half, pl.ds(y, 54, stride=8), :]
        for r in (1, 7, 2, 6, 3, 5, 4):
            d_cps[half][r].wait_recv()
            total = total + drecv[half, r - 1, 0:54].astype(F32)
        ssum[half] = total
        for h in range(2):
            got = ssum[half, pl.ds(h, 27, stride=2), :]
            zsend[half, h] = jnp.concatenate([got, jnp.zeros((5, 128), F32)], axis=0).astype(BF)
        for h in range(2):
            for l in range(3):
                tz = 2 * c + h
                i = counter[0]
                counter[0] += 1
                away = jnp.logical_or(tz != zh, zl != l)
                cp = pltpu.make_async_remote_copy(
                    src_ref=zsend.at[half, h], dst_ref=zrecv.at[half, myz], send_sem=send_sem.at[i],
                    recv_sem=recv_sem.at[zbase + half * NZ + myz], device_id=at_z(l, tz),
                    device_id_type=pl.DeviceIdType.MESH,
                )
                pl.when(away)(cp.start)
                zsends.append((away, cp))

    for cp in ug_cps:
        cp.wait_recv()
    for k in range(NM):
        rows = min(PIECE, 432 - k * PIECE)
        out_up[k * PIECE : k * PIECE + rows, :] = ufin[k, 0:rows]

    xbase = counter[0]
    counter[0] += 2 * NX
    xsends = []
    for half in range(2):

        @pl.when(home)
        def _():
            zrecv[half, myz] = zsend[half, zh - 2 * c]

        for j in range(NZ):
            cp = pltpu.make_async_remote_copy(
                src_ref=zsend.at[half, 0], dst_ref=zrecv.at[half, j], send_sem=send_sem.at[zbase + half * NZ + j],
                recv_sem=recv_sem.at[zbase + half * NZ + j], device_id=at_z(zl, zh),
                device_id_type=pl.DeviceIdType.MESH,
            )
            pl.when(jnp.logical_and(home, myz != j))(cp.wait_recv)

        @pl.when(home)
        def _():
            done = zrecv[half, 0].astype(F32)
            for j in range(1, NZ):
                done = done + zrecv[half, j].astype(F32)
            xrecv[half, x] = done * (1.0 / 24.0)

        for r in range(1, NM):
            i = counter[0]
            counter[0] += 1
            cp = pltpu.make_async_remote_copy(
                src_ref=xrecv.at[half, x], dst_ref=xrecv.at[half, x], send_sem=send_sem.at[i],
                recv_sem=recv_sem.at[xbase + half * NX + x], device_id=at_m(r),
                device_id_type=pl.DeviceIdType.MESH,
            )
            pl.when(home)(cp.start)
            xsends.append(cp)
    for half in range(2):
        for k in range(NX):
            cp = pltpu.make_async_remote_copy(
                src_ref=xrecv.at[half, k], dst_ref=xrecv.at[half, k], send_sem=send_sem.at[xbase + half * NX + k],
                recv_sem=recv_sem.at[xbase + half * NX + k], device_id=mate,
                device_id_type=pl.DeviceIdType.MESH,
            )
            pl.when(jnp.logical_not(jnp.logical_and(home, x == k)))(cp.wait_recv)
        for k in range(NX):
            out_low[:, k, 128 * half : 128 * half + 128] = xrecv[half, k, 0:27]

    for cp in pending:
        cp.wait_send()
    for away, cp in zsends:
        pl.when(away)(cp.wait_send)
    for cp in xsends:
        pl.when(home)(cp.wait_send)


def body(act_64, cot_32, filters_32, act_128):
    consts = [jnp.asarray(t, BF) for t in tables()]
    consts[1] = consts[1].astype(F32)[:64, :64]
    act = act_64.reshape(64 * 64, 256)
    cot = cot_32[0].transpose(1, 2, 3, 0).reshape(256, 32)
    filt = filters_32.transpose(0, 1, 2, 4, 3).reshape(27, 16, 256)
    low = act_128.reshape(4, 256, 128)
    operands = (act, cot, filt, low, *consts)
    vm = pltpu.VMEM
    up, lowg, cot_full = pl.pallas_call(
        kernel,
        out_shape=(
            jax.ShapeDtypeStruct((432, 256), F32),
            jax.ShapeDtypeStruct((27, 4, 256), F32),
            jax.ShapeDtypeStruct((128, 256), F32),
        ),
        in_specs=[pl.BlockSpec(memory_space=pltpu.HBM)] * 10,
        out_specs=[pl.BlockSpec(memory_space=pltpu.VMEM)] * 3,
        scratch_shapes=[
            vm(act.shape, BF), vm(cot.shape, BF), vm((4, 2, 28, 16, 128), BF), vm(low.shape, BF),
            *[vm(t.shape, t.dtype) for t in consts],
            vm((528, 128), F32), vm((4, 128, 128), BF), vm((4, 128, 128), BF), vm((8, 512, 256), BF),
            vm((448, 256), F32), vm((7, PIECE, 256), F32), vm((3, PIECE, 256), F32), vm((NM, PIECE, 256), F32),
            vm((2, 512, 256), BF), vm((8, 8, 16, 256), F32), vm((4, 8, 16, 256), F32), vm((3, 8, 16, 256), F32),
            vm((256, 128), BF), vm((5, 128, 256), BF), vm((384, 512), BF),
            vm((NM, 27, 16, 128), BF), vm((NM, 27, 16, 128), BF),
            vm((NM, 2, 64, 256), BF), vm((2, 432, 128), F32),
            vm((2, 8, 64, 128), BF), vm((2, 7, 64, 128), BF), vm((2, 54, 128), F32),
            vm((2, 2, 32, 128), BF), vm((2, NZ, 32, 128), BF), vm((2, NX, 32, 128), F32),
            pltpu.SemaphoreType.DMA((16,)), pltpu.SemaphoreType.DMA((192,)), pltpu.SemaphoreType.DMA((192,)),
        ],
        compiler_params=pltpu.CompilerParams(
            collective_id=0, has_side_effects=True, vmem_limit_bytes=67043328
        ),
    )(*operands)
    up = up.reshape(3, 3, 3, 16, 256).transpose(0, 1, 2, 4, 3)
    return up, lowg.reshape(3, 3, 3, 4, 256), cot_full.reshape(1, 2, 8, 8, 256)


def solution(mesh):
    placed = (
        P("sample", None, None, None, None),
        P("sample", None, None, None, "chan"),
        P(None, None, None, None, "chan"),
        P("sample", "chan", None, None, None),
    )
    return jax.shard_map(
        body,
        mesh=mesh,
        in_specs=placed,
        out_specs=(
            P(None, None, None, None, "chan"),
            P(None, None, None, "chan", None),
            P("sample", "chan", None, None, None),
        ),
        check_vma=False,
    )
```

```python
import jax
import jax.numpy as jnp
import numpy as np
from jax import lax
from jax.experimental import pallas as pl
from jax.experimental.pallas import tpu as pltpu
from jax.sharding import PartitionSpec as P

leak_slope = 0.3
BF = jnp.bfloat16
F32 = jnp.float32
NX, NZL, NC = 4, 3, 2
NZH, NY = 4, 8
NM = NX * NC
NZ = NZH * NZL
PIECE = 56


def tap_of(par, shift):
    if par == 0:
        return 1 if shift == 0 else None
    return 2 if shift == 0 else 0


def class_taps(p):
    found = []
    for q in range(8):
        taps = [tap_of((p >> b) & 1, (q >> b) & 1) for b in (2, 1, 0)]
        if None not in taps:
            found.append((q, taps[0] * 9 + taps[1] * 3 + taps[2]))
    return found


def tables():
    split = np.zeros((256, 256), np.float32)
    for p in range(8):
        pz, py, px = p >> 2, (p >> 1) & 1, p & 1
        for a in range(2):
            for b in range(4):
                for c in range(4):
                    split[p * 32 + a * 16 + b * 4 + c, (2 * a + pz) * 64 + (2 * b + py) * 8 + 2 * c + px] = 1
    merge = np.zeros((128, 128), np.float32)
    for p in range(8):
        pz, py, px = p >> 2, (p >> 1) & 1, p & 1
        for b in range(4):
            for c in range(4):
                merge[pz * 64 + (2 * b + py) * 8 + 2 * c + px, p * 16 + b * 4 + c] = 1
    spread16 = np.zeros((16, 128), np.float32)
    for q in range(8):
        for f in range(16):
            spread16[f, q * 16 + f] = 1
    shift = np.zeros((128, 512), np.float32)
    for k in range(4):
        dy, dx = k >> 1, k & 1
        for a in range(8):
            for b in range(4 - dy):
                for c in range(4 - dx):
                    shift[a * 16 + b * 4 + c, k * 128 + a * 16 + (b + dy) * 4 + c + dx] = 1
    order = np.zeros((128, 128), np.float32)
    for m in range(NM):
        for h in range(2):
            for y in range(8):
                order[m * 16 + h * 8 + y, 4 * ((2 * (m % 2) + h) * 8 + y) + m // 2] = 1
    pick = np.zeros((9, 512, 128), np.float32)
    for j in range(3):
        for k in range(3):
            for z in range(2):
                for y in range(8):
                    for x in range(8):
                        row, col = 2 * y + j - 1, 2 * x + k - 1
                        if row >= 0 and col >= 0:
                            pick[j * 3 + k, z * 256 + row * 16 + col, z * 64 + y * 8 + x] = 1
    return split, merge, spread16, shift, order, pick, np.eye(256, dtype=np.float32), np.tile(spread16, (16, 1))


def mm(a, b):
    return jnp.dot(a, b, preferred_element_type=F32)


def kernel(
    act_hbm, cot_hbm, filt_hbm, low_hbm,
    split_hbm, merge_hbm, spread_hbm, shift_hbm, order_hbm, pick_hbm, eye_hbm, tall_hbm,
    out_up, out_low, out_cot,
    act_ref, cot_ref, fbuf, low_ref,
    split_ref, merge_ref, spread_ref, shift_ref, order_ref, pick_ref, eye_ref, tall_ref,
    wide_ref, wide_far, planes, qsend, qrecv, w_ref, wq_ref, a_ref, u_ref, urecv, uzl, ufin,
    r_ref, part, rlong, rshort,
    rim, t_ref, lstack, lsend, lrecv, call, res,
    dsend, drecv, ssum, zsend, zrecv, xrecv,
    load_sem, send_sem, recv_sem,
):
    s = lax.axis_index("sample")
    ch = lax.axis_index("chan")
    c = s % 2
    zl = (s // 2) % 3
    x = s // 6
    y = ch % 8
    zh = ch // 8
    m = x * 2 + c
    mate = (s + 1 - 2 * c, ch)

    def at_zh(d):
        return (s, lax.rem(zh + d, NZH) * 8 + y)

    def at_y(d):
        return (s, zh * 8 + lax.rem(y + d, NY))

    def m_at(r):
        return lax.rem(m + r, NM)

    def at_m(r):
        other = m_at(r)
        return (((other // 2) * 3 + zl) * 2 + other % 2, ch)

    def at_x(r):
        return ((lax.rem(x + r, NX) * 3 + zl) * 2 + c, ch)

    def from_x(r, core):
        return lax.rem(x + NX - r, NX) * 2 + core

    def at_z(zl_, zh_):
        return ((x * 3 + zl_) * 2 + c, zh_ * 8 + y)

    counter = [0]
    pending = []

    def remote(src, dst, dev):
        i = counter[0]
        counter[0] += 1
        cp = pltpu.make_async_remote_copy(
            src_ref=src, dst_ref=dst, send_sem=send_sem.at[i], recv_sem=recv_sem.at[i],
            device_id=dev, device_id_type=pl.DeviceIdType.MESH,
        )
        cp.start()
        pending.append(cp)
        return cp

    barrier = pltpu.get_barrier_semaphore()
    partners = [at_y(d) for d in range(1, 8)] + [at_m(r) for r in range(1, 8)]
    partners += [(s, lax.rem(ch + 1, 32)), (s, lax.rem(ch + 31, 32))]
    for dzl in range(3):
        for dzh in range(4):
            if dzl or dzh:
                partners.append(at_z(lax.rem(zl + dzl, 3), lax.rem(zh + dzh, 4)))
    for dev in partners:
        pl.semaphore_signal(barrier, inc=1, device_id=dev, device_id_type=pl.DeviceIdType.MESH)

    loads = {}
    for i, (name, src, dst) in enumerate((
        ("f0", filt_hbm.at[:, :, 0:128], fbuf.at[0, 0, 0:27]), ("f1", filt_hbm.at[:, :, 128:256], fbuf.at[0, 1, 0:27]),
        ("cot", cot_hbm, cot_ref), ("eye", eye_hbm, eye_ref), ("low", low_hbm, low_ref),
        ("spread", spread_hbm, spread_ref), ("shift", shift_hbm, shift_ref), ("tall", tall_hbm, tall_ref),
        ("split", split_hbm, split_ref), ("act", act_hbm, act_ref),
        ("order", order_hbm, order_ref), ("pick", pick_hbm, pick_ref), ("merge", merge_hbm, merge_ref),
    )):
        cp = pltpu.make_async_copy(src, dst, load_sem.at[i])
        cp.start()
        loads[name] = cp
    fbuf[0, :, 27] = jnp.zeros((2, 16, 128), BF)

    loads["cot"].wait()
    loads["eye"].wait()
    planes[0:32, :] = lax.dot_general(
        cot_ref[...], eye_ref[...], (((0,), (0,)), ((), ())), preferred_element_type=F32
    )
    planes[32:40, :] = jnp.zeros((8, 256), F32)
    for q in range(4):
        qsend[q] = planes[8 * q : 8 * q + 16, :].astype(BF)
    for name in ("f0", "f1", "low"):
        loads[name].wait()

    pl.semaphore_wait(barrier, len(partners))

    share = pl.ds(7 * x, 7)
    f_z = {}
    for d in (2, 1, 3):
        f_z[d] = remote(fbuf.at[0, c, share], fbuf.at[4 - d, c, share], at_zh(d))
    q_cps = []
    for d in (2, 1, 3):
        q_cps.append(remote(qsend.at[lax.rem(zh + d, NZH)], qrecv.at[3 - d], at_zh(d)))
    rim_cp = remote(low_ref.at[3], rim, (s, lax.rem(ch + 1, 32)))

    lane = lax.broadcasted_iota(jnp.int32, (128, 128), 1) // 16

    def shifted(near, far):
        both = jnp.where(lane >= 4, far, near)
        terms = [jnp.where(lane % 4 == k, both, 0.0).astype(BF) for k in range(4)]
        return mm(shift_ref[...], jnp.concatenate(terms, axis=0)).astype(BF)

    loads["spread"].wait()
    loads["shift"].wait()
    for bc in range(16):
        got = lax.dot_general(
            cot_ref[bc * 16 : bc * 16 + 16, :], spread_ref[...], (((0,), (0,)), ((), ())), preferred_element_type=F32
        )
        wide_ref[pl.ds(bc, 32, stride=16), :] = got
    wide_ref[512:528, :] = jnp.zeros((16, 128), F32)
    for g in range(4):
        w_ref[g] = shifted(wide_ref[128 * g : 128 * g + 128, :], wide_ref[128 * g + 16 : 128 * g + 144, :])

    loads["split"].wait()
    loads["act"].wait()

    def split_group(g, carry):
        got = mm(split_ref[...], act_ref[pl.ds(pl.multiple_of(g * 256, 256), 256), :]).astype(BF)
        for p in range(8):
            a_ref[p, pl.ds(pl.multiple_of(g * 32, 32), 32), :] = got[p * 32 : p * 32 + 32]
        return carry

    lax.fori_loop(0, 16, split_group, 0)

    f_x = {}
    f_c = {}

    def spread_x(d):
        f_z[d].wait_recv()
        f_x[d] = [remote(fbuf.at[4 - d, c, share], fbuf.at[4 - d, c, share], at_x(r)) for r in (2, 1, 3)]

    def spread_c(d):
        for cp in f_x[d]:
            cp.wait_recv()
        f_c[d] = remote(fbuf.at[4 - d, c], fbuf.at[4 - d, c], mate)

    spread_x(1)
    spread_x(3)

    wt = jnp.concatenate([jnp.transpose(w_ref[g].astype(F32)) for g in range(4)], axis=1).astype(BF)
    for p in range(8):
        got = mm(wt, a_ref[p])
        for q, tap in class_taps(p):
            u_ref[tap * 16 : tap * 16 + 16, :] = got[q * 16 : q * 16 + 16]
    u_ref[432:448, :] = jnp.zeros((16, 256), F32)
    spread_x(2)
    spread_c(1)
    spread_c(3)
    u_cps = []
    for r in range(1, NM):
        u_cps.append(remote(u_ref.at[pl.ds(m_at(r) * PIECE, PIECE)], urecv.at[r - 1], at_m(r)))

    loads["order"].wait()
    loads["pick"].wait()
    rim_cp.wait_recv()
    edge = rim[...]
    edge = jnp.where(ch == 0, jnp.zeros_like(edge), edge)
    for q in range(5):
        plane = edge if q == 0 else low_ref[q - 1]
        got = lax.dot_general(order_ref[...], plane, (((1,), (1,)), ((), ())), preferred_element_type=F32)
        t_ref[q] = got.astype(BF)
    for i in range(3):
        lstack[i * 128 : i * 128 + 128, 0:256] = t_ref[i]
        lstack[i * 128 : i * 128 + 128, 256:512] = t_ref[i + 2]
    spread_c(2)

    loads["tall"].wait()
    for cp in q_cps:
        cp.wait_recv()
    wq_ref[0] = w_ref[zh]
    group = lax.broadcasted_iota(jnp.int32, (48, 256), 1) // 16
    rows = jnp.concatenate([qrecv[0], qrecv[1], qrecv[2]], axis=0).astype(F32)
    for bc in range(16):
        got = mm(jnp.where(group == bc, rows, 0.0).astype(BF), tall_ref[...])
        for r in range(3):
            wide_far[r, pl.ds(bc, 16, stride=16), :] = got[r * 16 : r * 16 + 16]
    for r in range(3):
        wq_ref[r + 1] = shifted(wide_far[r, 0:128, :], wide_far[r, 16:144, :])
    left = jnp.concatenate([wq_ref[r] for r in range(4)], axis=1)
    for d in (1, 3, 2):
        f_c[d].wait_recv()

    def partial(p):
        taps = dict(class_taps(p))
        for r in range(4):
            for q in range(8):
                row = r * 128 + q * 16
                for half in range(2):
                    lanes = slice(128 * half, 128 * half + 128)
                    if q in taps:
                        r_ref[p % 2, row : row + 16, lanes] = fbuf[r, half, taps[q]]
                    else:
                        r_ref[p % 2, row : row + 16, lanes] = jnp.zeros((16, 128), BF)
        got = mm(left, r_ref[p % 2])
        for k in range(8):
            part[k, p] = got[k * 16 : k * 16 + 16]

    halves = (pl.ds(0, 4), pl.ds(4, 4))
    way = (1, 7)
    back = (7, 1)
    longs = [[None] * 2 for _ in range(4)]
    shorts = [[None] * 2 for _ in range(3)]

    def ring(t, h):
        o = lax.rem(y + way[h] * (4 - t), NY)
        if t:
            longs[t - 1][h].wait_recv()
            part[o, halves[h]] = part[o, halves[h]] + rlong[t - 1, halves[h]]
        longs[t][h] = remote(part.at[o, halves[h]], rlong.at[t, halves[h]], at_y(way[h]))
        if t < 3:
            o = lax.rem(y + back[h] * (3 - t), NY)
            if t:
                shorts[t - 1][h].wait_recv()
                part[o, halves[h]] = part[o, halves[h]] + rshort[t - 1, halves[h]]
            shorts[t][h] = remote(part.at[o, halves[h]], rshort.at[t, halves[h]], at_y(back[h]))

    for p in range(4):
        partial(p)
    ring(0, 0)
    for p in range(4, 8):
        partial(p)
    ring(0, 1)

    def window(jk, carry):
        got = mm(lstack[...], pick_ref[jk]).astype(BF)
        for i in range(3):
            for k in range(NM):
                lsend[k, i * 9 + jk] = got[i * 128 + k * 16 : i * 128 + k * 16 + 16]
        return carry

    lax.fori_loop(0, 3, window, 0)
    ring(1, 0)
    ring(1, 1)
    lax.fori_loop(3, 9, window, 0)
    l_cps = []
    for r in range(1, NM):
        l_cps.append(remote(lsend.at[m_at(r)], lrecv.at[m], at_m(r)))
    ring(2, 0)
    ring(2, 1)
    piece = u_ref[pl.ds(pl.multiple_of(m * PIECE, 8), PIECE), :]
    for r in range(1, NM):
        u_cps[r - 1].wait_recv()
        piece = piece + urecv[r - 1]
    uzl[zl] = piece
    uz_cps = []
    for d in (1, 2):
        uz_cps.append(remote(uzl.at[zl], uzl.at[zl], at_z(lax.rem(zl + d, 3), zh)))
    ring(3, 0)
    ring(3, 1)

    loads["merge"].wait()
    c_x = [[None] * 4 for _ in range(2)]
    c_m = [None] * 2
    for h in range(2):
        shorts[2][h].wait_recv()
        longs[3][h].wait_recv()
        total = part[y, halves[h]] + rlong[3, halves[h]] + rshort[2, halves[h]]
        total = total.reshape(64, 256)
        natural = jnp.dot(merge_ref[...], total, preferred_element_type=F32, precision=lax.Precision.HIGHEST)
        own = act_ref[pl.ds(pl.multiple_of(ch * 128 + h * 64, 64), 64), :].astype(F32)
        cot = natural * jnp.where(own > 0, 1.0, leak_slope)
        out_cot[h * 64 : h * 64 + 64, :] = cot
        call[m, h] = cot.astype(BF)
        for r in (2, 1, 3):
            c_x[h][r] = remote(call.at[m, h], call.at[m, h], at_x(r))
        c_m[h] = remote(call.at[m, h], call.at[m, h], mate)

    def term(lhs, src):
        rhs = jnp.concatenate([call[src, 0], call[src, 1]], axis=0)
        return mm(lhs.reshape(432, 128), rhs)

    acc = term(lsend[m], m)
    for cp in l_cps:
        cp.wait_recv()
    c_f = [[None] * 4 for _ in range(2)]
    for h in range(2):
        for r in (1, 3, 2):
            c_x[h][r].wait_recv()
            got = from_x(r, c)
            c_f[h][r] = remote(call.at[got, h], call.at[got, h], mate)
    for h in range(2):
        c_m[h].wait_recv()
    acc = acc + term(lrecv[x * 2 + 1 - c], x * 2 + 1 - c)
    for r in (1, 3, 2):
        acc = acc + term(lrecv[from_x(r, c)], from_x(r, c))
    for cp in uz_cps:
        cp.wait_recv()
    ufin[m] = (uzl[0] + uzl[1] + uzl[2]) * (1.0 / 24.0)
    for r in (1, 3, 2):
        for h in range(2):
            c_f[h][r].wait_recv()
        acc = acc + term(lrecv[from_x(r, 1 - c)], from_x(r, 1 - c))
    for half in range(2):
        res[half] = acc[:, 128 * half : 128 * half + 128]

    d_cps = [[None] * NY for _ in range(2)]
    for half in range(2):
        for k in range(NY):
            got = res[half, pl.ds(k, 54, stride=8), :].astype(BF)
            dsend[half, k] = jnp.concatenate([got, jnp.zeros((10, 128), BF)], axis=0)
        for r in (4, 3, 5, 2, 6, 1, 7):
            d_cps[half][r] = remote(dsend.at[half, lax.rem(y + r, NY)], drecv.at[half, r - 1], at_y(r))
    ug_cps = []
    for r in range(1, NM):
        ug_cps.append(remote(ufin.at[m], ufin.at[m], at_m(r)))

    myz = zh * 3 + zl
    home = zh // 2 == c
    zbase = counter[0]
    counter[0] += 2 * NZ
    zsends = []
    for half in range(2):
        total = res[half, pl.ds(y, 54, stride=8), :]
        for r in (1, 7, 2, 6, 3, 5, 4):
            d_cps[half][r].wait_recv()
            total = total + drecv[half, r - 1, 0:54].astype(F32)
        ssum[half] = total
        for h in range(2):
            got = ssum[half, pl.ds(h, 27, stride=2), :]
            zsend[half, h] = jnp.concatenate([got, jnp.zeros((5, 128), F32)], axis=0).astype(BF)
        for h in range(2):
            for l in range(3):
                tz = 2 * c + h
                i = counter[0]
                counter[0] += 1
                away = jnp.logical_or(tz != zh, zl != l)
                cp = pltpu.make_async_remote_copy(
                    src_ref=zsend.at[half, h], dst_ref=zrecv.at[half, myz], send_sem=send_sem.at[i],
                    recv_sem=recv_sem.at[zbase + half * NZ + myz], device_id=at_z(l, tz),
                    device_id_type=pl.DeviceIdType.MESH,
                )
                pl.when(away)(cp.start)
                zsends.append((away, cp))

    for cp in ug_cps:
        cp.wait_recv()
    for k in range(NM):
        rows = min(PIECE, 432 - k * PIECE)
        out_up[k * PIECE : k * PIECE + rows, :] = ufin[k, 0:rows]

    xbase = counter[0]
    counter[0] += 2 * NX
    xsends = []
    for half in range(2):

        @pl.when(home)
        def _():
            zrecv[half, myz] = zsend[half, zh - 2 * c]

        for j in range(NZ):
            cp = pltpu.make_async_remote_copy(
                src_ref=zsend.at[half, 0], dst_ref=zrecv.at[half, j], send_sem=send_sem.at[zbase + half * NZ + j],
                recv_sem=recv_sem.at[zbase + half * NZ + j], device_id=at_z(zl, zh),
                device_id_type=pl.DeviceIdType.MESH,
            )
            pl.when(jnp.logical_and(home, myz != j))(cp.wait_recv)

        @pl.when(home)
        def _():
            done = zrecv[half, 0].astype(F32)
            for j in range(1, NZ):
                done = done + zrecv[half, j].astype(F32)
            xrecv[half, x] = done * (1.0 / 24.0)

        for r in range(1, NM):
            i = counter[0]
            counter[0] += 1
            cp = pltpu.make_async_remote_copy(
                src_ref=xrecv.at[half, x], dst_ref=xrecv.at[half, x], send_sem=send_sem.at[i],
                recv_sem=recv_sem.at[xbase + half * NX + x], device_id=at_m(r),
                device_id_type=pl.DeviceIdType.MESH,
            )
            pl.when(home)(cp.start)
            xsends.append(cp)
    for half in range(2):
        for k in range(NX):
            cp = pltpu.make_async_remote_copy(
                src_ref=xrecv.at[half, k], dst_ref=xrecv.at[half, k], send_sem=send_sem.at[xbase + half * NX + k],
                recv_sem=recv_sem.at[xbase + half * NX + k], device_id=mate,
                device_id_type=pl.DeviceIdType.MESH,
            )
            pl.when(jnp.logical_not(jnp.logical_and(home, x == k)))(cp.wait_recv)
        for k in range(NX):
            out_low[:, k, 128 * half : 128 * half + 128] = xrecv[half, k, 0:27]

    for cp in pending:
        cp.wait_send()
    for away, cp in zsends:
        pl.when(away)(cp.wait_send)
    for cp in xsends:
        pl.when(home)(cp.wait_send)


def flush(a, b, c, out_a, out_b, out_c, sem):
    moves = [pltpu.make_async_copy(src, dst, sem.at[i]) for i, (src, dst) in enumerate(((a, out_a), (b, out_b), (c, out_c)))]
    for cp in moves:
        cp.start()
    for cp in moves:
        cp.wait()


def body(act_64, cot_32, filters_32, act_128):
    consts = [jnp.asarray(t, BF) for t in tables()]
    consts[1] = consts[1].astype(F32)[:64, :64]
    act = act_64.reshape(64 * 64, 256)
    cot = cot_32[0].transpose(1, 2, 3, 0).reshape(256, 32)
    filt = filters_32.transpose(0, 1, 2, 4, 3).reshape(27, 16, 256)
    low = act_128.reshape(4, 256, 128)
    operands = [pltpu.with_memory_space_constraint(t, pltpu.HBM) for t in (act, cot, filt, low, *consts)]
    vm = pltpu.VMEM
    up, lowg, cot_full = pl.pallas_call(
        kernel,
        out_shape=(
            jax.ShapeDtypeStruct((432, 256), F32),
            jax.ShapeDtypeStruct((27, 4, 256), F32),
            jax.ShapeDtypeStruct((128, 256), F32),
        ),
        in_specs=[pl.BlockSpec(memory_space=pltpu.HBM)] * len(operands),
        out_specs=[pl.BlockSpec(memory_space=pltpu.VMEM)] * 3,
        scratch_shapes=[
            vm(act.shape, BF), vm(cot.shape, BF), vm((4, 2, 28, 16, 128), BF), vm(low.shape, BF),
            *[vm(t.shape, t.dtype) for t in consts],
            vm((528, 128), F32), vm((3, 256, 128), F32), vm((40, 256), F32), vm((4, 16, 256), BF), vm((3, 16, 256), BF),
            vm((4, 128, 128), BF), vm((4, 128, 128), BF), vm((8, 512, 256), BF),
            vm((448, 256), F32), vm((7, PIECE, 256), F32), vm((3, PIECE, 256), F32), vm((NM, PIECE, 256), F32),
            vm((2, 512, 256), BF), vm((8, 8, 16, 256), F32), vm((4, 8, 16, 256), F32), vm((3, 8, 16, 256), F32),
            vm((256, 128), BF), vm((5, 128, 256), BF), vm((384, 512), BF),
            vm((NM, 27, 16, 128), BF), vm((NM, 27, 16, 128), BF),
            vm((NM, 2, 64, 256), BF), vm((2, 432, 128), F32),
            vm((2, 8, 64, 128), BF), vm((2, 7, 64, 128), BF), vm((2, 54, 128), F32),
            vm((2, 2, 32, 128), BF), vm((2, NZ, 32, 128), BF), vm((2, NX, 32, 128), F32),
            pltpu.SemaphoreType.DMA((16,)), pltpu.SemaphoreType.DMA((192,)), pltpu.SemaphoreType.DMA((192,)),
        ],
        compiler_params=pltpu.CompilerParams(
            collective_id=0, has_side_effects=True, vmem_limit_bytes=48 * 1024 * 1024
        ),
    )(*operands)
    up, lowg, cot_full = pl.pallas_call(
        flush,
        out_shape=tuple(jax.ShapeDtypeStruct(t.shape, t.dtype) for t in (up, lowg, cot_full)),
        in_specs=[pl.BlockSpec(memory_space=pltpu.VMEM)] * 3,
        out_specs=[pl.BlockSpec(memory_space=pltpu.HBM)] * 3,
        scratch_shapes=[pltpu.SemaphoreType.DMA((3,))],
        compiler_params=pltpu.CompilerParams(vmem_limit_bytes=8 * 1024 * 1024),
    )(up, lowg, cot_full)
    up = up.reshape(3, 3, 3, 16, 256).transpose(0, 1, 2, 4, 3)
    return up, lowg.reshape(3, 3, 3, 4, 256), cot_full.reshape(1, 2, 8, 8, 256)


def solution(mesh):
    placed = (
        P("sample", None, None, None, None),
        P("sample", None, None, None, "chan"),
        P(None, None, None, None, "chan"),
        P("sample", "chan", None, None, None),
    )
    return jax.shard_map(
        body,
        mesh=mesh,
        in_specs=placed,
        out_specs=(
            P(None, None, None, None, "chan"),
            P(None, None, None, "chan", None),
            P("sample", "chan", None, None, None),
        ),
        check_vma=False,
    )
```

```python
import jax
import jax.numpy as jnp
import numpy as np
from jax import lax
from jax.experimental import pallas as pl
from jax.experimental.pallas import tpu as pltpu
from jax.sharding import PartitionSpec as P

leak_slope = 0.3
BF = jnp.bfloat16
F32 = jnp.float32
NX, NZL, NC = 4, 3, 2
NZH, NY = 4, 8
NM = NX * NC
NZ = NZH * NZL
PIECE = 56


def tap_of(par, shift):
    if par == 0:
        return 1 if shift == 0 else None
    return 2 if shift == 0 else 0


def class_taps(p):
    found = []
    for q in range(8):
        taps = [tap_of((p >> b) & 1, (q >> b) & 1) for b in (2, 1, 0)]
        if None not in taps:
            found.append((q, taps[0] * 9 + taps[1] * 3 + taps[2]))
    return found


def tables():
    split = np.zeros((256, 256), np.float32)
    for p in range(8):
        pz, py, px = p >> 2, (p >> 1) & 1, p & 1
        for a in range(2):
            for b in range(4):
                for c in range(4):
                    split[p * 32 + a * 16 + b * 4 + c, (2 * a + pz) * 64 + (2 * b + py) * 8 + 2 * c + px] = 1
    merge = np.zeros((128, 128), np.float32)
    for p in range(8):
        pz, py, px = p >> 2, (p >> 1) & 1, p & 1
        for b in range(4):
            for c in range(4):
                merge[pz * 64 + (2 * b + py) * 8 + 2 * c + px, p * 16 + b * 4 + c] = 1
    spread16 = np.zeros((16, 128), np.float32)
    for q in range(8):
        for f in range(16):
            spread16[f, q * 16 + f] = 1
    shift = np.zeros((128, 512), np.float32)
    for k in range(4):
        dy, dx = k >> 1, k & 1
        for a in range(8):
            for b in range(4 - dy):
                for c in range(4 - dx):
                    shift[a * 16 + b * 4 + c, k * 128 + a * 16 + (b + dy) * 4 + c + dx] = 1
    order = np.zeros((128, 128), np.float32)
    for m in range(NM):
        for h in range(2):
            for y in range(8):
                order[m * 16 + h * 8 + y, 4 * ((2 * (m % 2) + h) * 8 + y) + m // 2] = 1
    pick = np.zeros((9, 512, 128), np.float32)
    for j in range(3):
        for k in range(3):
            for z in range(2):
                for y in range(8):
                    for x in range(8):
                        row, col = 2 * y + j - 1, 2 * x + k - 1
                        if row >= 0 and col >= 0:
                            pick[j * 3 + k, z * 256 + row * 16 + col, z * 64 + y * 8 + x] = 1
    return split, merge, spread16, shift, order, pick, np.eye(256, dtype=np.float32), np.tile(spread16, (16, 1))


def mm(a, b):
    return jnp.dot(a, b, preferred_element_type=F32)


def kernel(
    act_hbm, cot_hbm, filt_hbm, low_hbm,
    split_hbm, merge_hbm, spread_hbm, shift_hbm, order_hbm, pick_hbm, eye_hbm, tall_hbm,
    out_up, out_low, out_cot,
    act_ref, cot_ref, fbuf, low_ref,
    split_ref, merge_ref, spread_ref, shift_ref, order_ref, pick_ref, eye_ref, tall_ref,
    wide_ref, wide_far, planes, qsend, qrecv, w_ref, wq_ref, a_ref, u_ref, urecv, uzl, ufin,
    r_ref, part, rlong, rshort,
    rim, t_ref, lstack, lsend, lrecv, call, res,
    dsend, drecv, ssum, zsend, zrecv, xrecv,
    load_sem, send_sem, recv_sem,
):
    s = lax.axis_index("sample")
    ch = lax.axis_index("chan")
    c = s % 2
    zl = (s // 2) % 3
    x = s // 6
    y = ch % 8
    zh = ch // 8
    m = x * 2 + c
    mate = (s + 1 - 2 * c, ch)

    def at_zh(d):
        return (s, jnp.bitwise_and(zh + d, NZH - 1) * 8 + y)

    def at_y(d):
        return (s, zh * 8 + jnp.bitwise_and(y + d, NY - 1))

    def m_at(r):
        return jnp.bitwise_and(m + r, NM - 1)

    def at_m(r):
        other = m_at(r)
        return (((other // 2) * 3 + zl) * 2 + other % 2, ch)

    def at_x(r):
        return ((jnp.bitwise_and(x + r, NX - 1) * 3 + zl) * 2 + c, ch)

    def from_x(r, core):
        return jnp.bitwise_and(x + NX - r, NX - 1) * 2 + core

    def at_z(zl_, zh_):
        return ((x * 3 + zl_) * 2 + c, zh_ * 8 + y)

    counter = [0]
    pending = []

    def remote(src, dst, dev):
        i = counter[0]
        counter[0] += 1
        cp = pltpu.make_async_remote_copy(
            src_ref=src, dst_ref=dst, send_sem=send_sem.at[i], recv_sem=recv_sem.at[i],
            device_id=dev, device_id_type=pl.DeviceIdType.MESH,
        )
        cp.start()
        pending.append(cp)
        return cp

    barrier = pltpu.get_barrier_semaphore()
    partners = [at_y(d) for d in range(1, 8)] + [at_m(r) for r in range(1, 8)]
    partners += [(s, lax.rem(ch + 1, 32)), (s, lax.rem(ch + 31, 32))]
    for dzl in range(3):
        for dzh in range(4):
            if dzl or dzh:
                partners.append(at_z(lax.rem(zl + dzl, 3), jnp.bitwise_and(zh + dzh, 3)))
    for dev in partners:
        pl.semaphore_signal(barrier, inc=1, device_id=dev, device_id_type=pl.DeviceIdType.MESH)

    loads = {}
    for i, (name, src, dst) in enumerate((
        ("f0", filt_hbm.at[:, :, 0:128], fbuf.at[0, 0, 0:27]), ("f1", filt_hbm.at[:, :, 128:256], fbuf.at[0, 1, 0:27]),
        ("cot", cot_hbm, cot_ref), ("eye", eye_hbm, eye_ref), ("low", low_hbm, low_ref),
        ("spread", spread_hbm, spread_ref), ("shift", shift_hbm, shift_ref), ("tall", tall_hbm, tall_ref),
        ("split", split_hbm, split_ref), ("act", act_hbm, act_ref),
        ("order", order_hbm, order_ref), ("pick", pick_hbm, pick_ref), ("merge", merge_hbm, merge_ref),
    )):
        cp = pltpu.make_async_copy(src, dst, load_sem.at[i])
        cp.start()
        loads[name] = cp
    fbuf[0, :, 27] = jnp.zeros((2, 16, 128), BF)

    loads["cot"].wait()
    loads["eye"].wait()
    planes[0:32, :] = lax.dot_general(
        cot_ref[...], eye_ref[...], (((0,), (0,)), ((), ())), preferred_element_type=F32
    )
    planes[32:40, :] = jnp.zeros((8, 256), F32)
    for q in range(4):
        qsend[q] = planes[8 * q : 8 * q + 16, :].astype(BF)
    for name in ("f0", "f1", "low"):
        loads[name].wait()

    pl.semaphore_wait(barrier, len(partners))

    share = pl.ds(7 * x, 7)
    f_z = {}
    for d in (2, 1, 3):
        f_z[d] = remote(fbuf.at[0, c, share], fbuf.at[4 - d, c, share], at_zh(d))
    q_cps = []
    for d in (2, 1, 3):
        q_cps.append(remote(qsend.at[jnp.bitwise_and(zh + d, NZH - 1)], qrecv.at[3 - d], at_zh(d)))
    rim_cp = remote(low_ref.at[3], rim, (s, lax.rem(ch + 1, 32)))

    lane = lax.broadcasted_iota(jnp.int32, (128, 128), 1) // 16

    def shifted(near, far):
        both = jnp.where(lane >= 4, far, near)
        terms = [jnp.where(lane % 4 == k, both, 0.0).astype(BF) for k in range(4)]
        return mm(shift_ref[...], jnp.concatenate(terms, axis=0)).astype(BF)

    loads["spread"].wait()
    loads["shift"].wait()
    for bc in range(16):
        got = lax.dot_general(
            cot_ref[bc * 16 : bc * 16 + 16, :], spread_ref[...], (((0,), (0,)), ((), ())), preferred_element_type=F32
        )
        wide_ref[pl.ds(bc, 32, stride=16), :] = got
    wide_ref[512:528, :] = jnp.zeros((16, 128), F32)
    for g in range(4):
        w_ref[g] = shifted(wide_ref[128 * g : 128 * g + 128, :], wide_ref[128 * g + 16 : 128 * g + 144, :])

    loads["split"].wait()
    loads["act"].wait()

    def split_group(g, carry):
        got = mm(split_ref[...], act_ref[pl.ds(pl.multiple_of(g * 256, 256), 256), :]).astype(BF)
        for p in range(8):
            a_ref[p, pl.ds(pl.multiple_of(g * 32, 32), 32), :] = got[p * 32 : p * 32 + 32]
        return carry

    lax.fori_loop(0, 16, split_group, 0)

    f_x = {}
    f_c = {}

    def spread_x(d):
        f_z[d].wait_recv()
        f_x[d] = [remote(fbuf.at[4 - d, c, share], fbuf.at[4 - d, c, share], at_x(r)) for r in (2, 1, 3)]

    def spread_c(d):
        for cp in f_x[d]:
            cp.wait_recv()
        f_c[d] = remote(fbuf.at[4 - d, c], fbuf.at[4 - d, c], mate)

    spread_x(1)
    spread_x(3)

    wt = jnp.concatenate([jnp.transpose(w_ref[g].astype(F32)) for g in range(4)], axis=1).astype(BF)
    for p in range(8):
        got = mm(wt, a_ref[p])
        for q, tap in class_taps(p):
            u_ref[tap * 16 : tap * 16 + 16, :] = got[q * 16 : q * 16 + 16]
    u_ref[432:448, :] = jnp.zeros((16, 256), F32)
    spread_x(2)
    loads["order"].wait()
    loads["pick"].wait()
    rim_cp.wait_recv()
    edge = rim[...]
    edge = jnp.where(ch == 0, jnp.zeros_like(edge), edge)
    for q in range(5):
        plane = edge if q == 0 else low_ref[q - 1]
        got = lax.dot_general(order_ref[...], plane, (((1,), (1,)), ((), ())), preferred_element_type=F32)
        t_ref[q] = got.astype(BF)
    for i in range(3):
        lstack[i * 128 : i * 128 + 128, 0:256] = t_ref[i]
        lstack[i * 128 : i * 128 + 128, 256:512] = t_ref[i + 2]
    spread_c(1)
    spread_c(3)

    def window(jk, carry):
        got = mm(lstack[...], pick_ref[jk]).astype(BF)
        for i in range(3):
            for k in range(NM):
                lsend[k, i * 9 + jk] = got[i * 128 + k * 16 : i * 128 + k * 16 + 16]
        return carry

    lax.fori_loop(0, 9, window, 0)
    spread_c(2)
    u_cps = []
    for r in range(1, NM):
        u_cps.append(remote(u_ref.at[pl.ds(m_at(r) * PIECE, PIECE)], urecv.at[r - 1], at_m(r)))

    l_cps = []
    for r in range(1, NM):
        l_cps.append(remote(lsend.at[m_at(r)], lrecv.at[m], at_m(r)))

    loads["tall"].wait()
    for cp in q_cps:
        cp.wait_recv()
    wq_ref[0] = w_ref[zh]
    group = lax.broadcasted_iota(jnp.int32, (48, 256), 1) // 16
    rows = jnp.concatenate([qrecv[0], qrecv[1], qrecv[2]], axis=0).astype(F32)
    for bc in range(16):
        got = mm(jnp.where(group == bc, rows, 0.0).astype(BF), tall_ref[...])
        for r in range(3):
            wide_far[r, pl.ds(bc, 16, stride=16), :] = got[r * 16 : r * 16 + 16]
    for r in range(3):
        wq_ref[r + 1] = shifted(wide_far[r, 0:128, :], wide_far[r, 16:144, :])
    left = jnp.concatenate([wq_ref[r] for r in range(4)], axis=1)
    for d in (1, 3, 2):
        f_c[d].wait_recv()

    def partial(p):
        taps = dict(class_taps(p))
        for r in range(4):
            for q in range(8):
                row = r * 128 + q * 16
                for half in range(2):
                    lanes = slice(128 * half, 128 * half + 128)
                    if q in taps:
                        r_ref[p % 2, row : row + 16, lanes] = fbuf[r, half, taps[q]]
                    else:
                        r_ref[p % 2, row : row + 16, lanes] = jnp.zeros((16, 128), BF)
        got = mm(left, r_ref[p % 2])
        for k in range(8):
            part[k, p] = got[k * 16 : k * 16 + 16]

    quarters = [pl.ds(2 * u, 2) for u in range(4)]
    way = (1, 7, 1, 7)
    back = (7, 1, 7, 1)
    longs = [[None] * 4 for _ in range(4)]
    shorts = [[None] * 4 for _ in range(3)]

    def ring(t, u):
        o = jnp.bitwise_and(y + way[u] * (4 - t), NY - 1)
        if t:
            longs[t - 1][u].wait_recv()
            part[o, quarters[u]] = part[o, quarters[u]] + rlong[t - 1, quarters[u]]
        longs[t][u] = remote(part.at[o, quarters[u]], rlong.at[t, quarters[u]], at_y(way[u]))
        if t < 3:
            o = jnp.bitwise_and(y + back[u] * (3 - t), NY - 1)
            if t:
                shorts[t - 1][u].wait_recv()
                part[o, quarters[u]] = part[o, quarters[u]] + rshort[t - 1, quarters[u]]
            shorts[t][u] = remote(part.at[o, quarters[u]], rshort.at[t, quarters[u]], at_y(back[u]))

    for u in range(4):
        partial(2 * u)
        partial(2 * u + 1)
        ring(0, u)
    for t in (1, 2):
        for u in range(4):
            ring(t, u)
    piece = u_ref[pl.ds(pl.multiple_of(m * PIECE, 8), PIECE), :]
    for r in range(1, NM):
        u_cps[r - 1].wait_recv()
        piece = piece + urecv[r - 1]
    uzl[zl] = piece
    uz_cps = []
    for d in (1, 2):
        uz_cps.append(remote(uzl.at[zl], uzl.at[zl], at_z(lax.rem(zl + d, 3), zh)))
    for u in range(4):
        ring(3, u)

    loads["merge"].wait()
    c_x = [[None] * 4 for _ in range(2)]
    c_m = [None] * 2
    for h in range(2):
        for u in (2 * h, 2 * h + 1):
            shorts[2][u].wait_recv()
            longs[3][u].wait_recv()
        both = pl.ds(4 * h, 4)
        total = part[y, both] + rlong[3, both] + rshort[2, both]
        total = total.reshape(64, 256)
        natural = jnp.dot(merge_ref[...], total, preferred_element_type=F32, precision=lax.Precision.HIGHEST)
        own = act_ref[pl.ds(pl.multiple_of(ch * 128 + h * 64, 64), 64), :].astype(F32)
        cot = natural * jnp.where(own > 0, 1.0, leak_slope)
        out_cot[h * 64 : h * 64 + 64, :] = cot
        call[m, h] = cot.astype(BF)
        for r in (2, 1, 3):
            c_x[h][r] = remote(call.at[m, h], call.at[m, h], at_x(r))
        c_m[h] = remote(call.at[m, h], call.at[m, h], mate)

    def terms(core):
        lhs = []
        rhs = []
        for r in range(NX):
            src = from_x(r, core)
            own = lsend[m] if r == 0 and core is c else lrecv[src]
            lhs.append(own.reshape(432, 128))
            rhs += [call[src, 0], call[src, 1]]
        return mm(jnp.concatenate(lhs, axis=1), jnp.concatenate(rhs, axis=0))

    for cp in l_cps:
        cp.wait_recv()
    c_f = [[None] * 4 for _ in range(2)]
    for h in range(2):
        for r in (1, 3, 2):
            c_x[h][r].wait_recv()
            got = from_x(r, c)
            c_f[h][r] = remote(call.at[got, h], call.at[got, h], mate)
    for cp in uz_cps:
        cp.wait_recv()
    ufin[m] = (uzl[0] + uzl[1] + uzl[2]) * (1.0 / 24.0)
    acc = terms(c)
    for h in range(2):
        c_m[h].wait_recv()
    for r in (1, 3, 2):
        for h in range(2):
            c_f[h][r].wait_recv()
    acc = acc + terms(1 - c)
    for half in range(2):
        res[half] = acc[:, 128 * half : 128 * half + 128]

    d_cps = [[None] * NY for _ in range(2)]
    for half in range(2):
        for k in range(NY):
            got = res[half, pl.ds(k, 54, stride=8), :].astype(BF)
            dsend[half, k] = jnp.concatenate([got, jnp.zeros((10, 128), BF)], axis=0)
        for r in (4, 3, 5, 2, 6, 1, 7):
            d_cps[half][r] = remote(dsend.at[half, jnp.bitwise_and(y + r, NY - 1)], drecv.at[half, r - 1], at_y(r))
    ug_cps = []
    for r in range(1, NM):
        ug_cps.append(remote(ufin.at[m], ufin.at[m], at_m(r)))

    myz = zh * 3 + zl
    home = zh // 2 == c
    zbase = counter[0]
    counter[0] += 2 * NZ
    zsends = []
    for half in range(2):
        total = res[half, pl.ds(y, 54, stride=8), :]
        for r in (1, 7, 2, 6, 3, 5, 4):
            d_cps[half][r].wait_recv()
            total = total + drecv[half, r - 1, 0:54].astype(F32)
        ssum[half] = total
        for h in range(2):
            got = ssum[half, pl.ds(h, 27, stride=2), :]
            zsend[half, h] = jnp.concatenate([got, jnp.zeros((5, 128), F32)], axis=0).astype(BF)
        for h in range(2):
            for l in range(3):
                tz = 2 * c + h
                i = counter[0]
                counter[0] += 1
                away = jnp.logical_or(tz != zh, zl != l)
                cp = pltpu.make_async_remote_copy(
                    src_ref=zsend.at[half, h], dst_ref=zrecv.at[half, myz], send_sem=send_sem.at[i],
                    recv_sem=recv_sem.at[zbase + half * NZ + myz], device_id=at_z(l, tz),
                    device_id_type=pl.DeviceIdType.MESH,
                )
                pl.when(away)(cp.start)
                zsends.append((away, cp))

    for cp in ug_cps:
        cp.wait_recv()
    for k in range(NM):
        rows = min(PIECE, 432 - k * PIECE)
        out_up[k * PIECE : k * PIECE + rows, :] = ufin[k, 0:rows]

    xbase = counter[0]
    counter[0] += 2 * NX
    xsends = []
    for half in range(2):

        @pl.when(home)
        def _():
            zrecv[half, myz] = zsend[half, zh - 2 * c]

        for j in range(NZ):
            cp = pltpu.make_async_remote_copy(
                src_ref=zsend.at[half, 0], dst_ref=zrecv.at[half, j], send_sem=send_sem.at[zbase + half * NZ + j],
                recv_sem=recv_sem.at[zbase + half * NZ + j], device_id=at_z(zl, zh),
                device_id_type=pl.DeviceIdType.MESH,
            )
            pl.when(jnp.logical_and(home, myz != j))(cp.wait_recv)

        @pl.when(home)
        def _():
            done = zrecv[half, 0].astype(F32)
            for j in range(1, NZ):
                done = done + zrecv[half, j].astype(F32)
            xrecv[half, x] = done * (1.0 / 24.0)

        for r in range(1, NM):
            i = counter[0]
            counter[0] += 1
            cp = pltpu.make_async_remote_copy(
                src_ref=xrecv.at[half, x], dst_ref=xrecv.at[half, x], send_sem=send_sem.at[i],
                recv_sem=recv_sem.at[xbase + half * NX + x], device_id=at_m(r),
                device_id_type=pl.DeviceIdType.MESH,
            )
            pl.when(home)(cp.start)
            xsends.append(cp)
    for half in range(2):
        for k in range(NX):
            cp = pltpu.make_async_remote_copy(
                src_ref=xrecv.at[half, k], dst_ref=xrecv.at[half, k], send_sem=send_sem.at[xbase + half * NX + k],
                recv_sem=recv_sem.at[xbase + half * NX + k], device_id=mate,
                device_id_type=pl.DeviceIdType.MESH,
            )
            pl.when(jnp.logical_not(jnp.logical_and(home, x == k)))(cp.wait_recv)
        for k in range(NX):
            out_low[:, k, 128 * half : 128 * half + 128] = xrecv[half, k, 0:27]

    for cp in pending:
        cp.wait_send()
    for away, cp in zsends:
        pl.when(away)(cp.wait_send)
    for cp in xsends:
        pl.when(home)(cp.wait_send)


def flush(a, b, c, out_a, out_b, out_c, sem):
    moves = [pltpu.make_async_copy(src, dst, sem.at[i]) for i, (src, dst) in enumerate(((a, out_a), (b, out_b), (c, out_c)))]
    for cp in moves:
        cp.start()
    for cp in moves:
        cp.wait()


def body(act_64, cot_32, filters_32, act_128):
    consts = [jnp.asarray(t, BF) for t in tables()]
    consts[1] = consts[1].astype(F32)[:64, :64]
    act = act_64.reshape(64 * 64, 256)
    cot = cot_32[0].transpose(1, 2, 3, 0).reshape(256, 32)
    filt = filters_32.transpose(0, 1, 2, 4, 3).reshape(27, 16, 256)
    low = act_128.reshape(4, 256, 128)
    operands = [pltpu.with_memory_space_constraint(t, pltpu.HBM) for t in (act, cot, filt, low, *consts)]
    vm = pltpu.VMEM
    up, lowg, cot_full = pl.pallas_call(
        kernel,
        out_shape=(
            jax.ShapeDtypeStruct((432, 256), F32),
            jax.ShapeDtypeStruct((27, 4, 256), F32),
            jax.ShapeDtypeStruct((128, 256), F32),
        ),
        in_specs=[pl.BlockSpec(memory_space=pltpu.HBM)] * len(operands),
        out_specs=[pl.BlockSpec(memory_space=pltpu.VMEM)] * 3,
        scratch_shapes=[
            vm(act.shape, BF), vm(cot.shape, BF), vm((4, 2, 28, 16, 128), BF), vm(low.shape, BF),
            *[vm(t.shape, t.dtype) for t in consts],
            vm((528, 128), F32), vm((3, 256, 128), F32), vm((40, 256), F32), vm((4, 16, 256), BF), vm((3, 16, 256), BF),
            vm((4, 128, 128), BF), vm((4, 128, 128), BF), vm((8, 512, 256), BF),
            vm((448, 256), F32), vm((7, PIECE, 256), F32), vm((3, PIECE, 256), F32), vm((NM, PIECE, 256), F32),
            vm((2, 512, 256), BF), vm((8, 8, 16, 256), F32), vm((4, 8, 16, 256), F32), vm((3, 8, 16, 256), F32),
            vm((256, 128), BF), vm((5, 128, 256), BF), vm((384, 512), BF),
            vm((NM, 27, 16, 128), BF), vm((NM, 27, 16, 128), BF),
            vm((NM, 2, 64, 256), BF), vm((2, 432, 128), F32),
            vm((2, 8, 64, 128), BF), vm((2, 7, 64, 128), BF), vm((2, 54, 128), F32),
            vm((2, 2, 32, 128), BF), vm((2, NZ, 32, 128), BF), vm((2, NX, 32, 128), F32),
            pltpu.SemaphoreType.DMA((16,)), pltpu.SemaphoreType.DMA((192,)), pltpu.SemaphoreType.DMA((192,)),
        ],
        compiler_params=pltpu.CompilerParams(
            collective_id=0, has_side_effects=True, vmem_limit_bytes=48 * 1024 * 1024
        ),
    )(*operands)
    up, lowg, cot_full = pl.pallas_call(
        flush,
        out_shape=tuple(jax.ShapeDtypeStruct(t.shape, t.dtype) for t in (up, lowg, cot_full)),
        in_specs=[pl.BlockSpec(memory_space=pltpu.VMEM)] * 3,
        out_specs=[pl.BlockSpec(memory_space=pltpu.HBM)] * 3,
        scratch_shapes=[pltpu.SemaphoreType.DMA((3,))],
        compiler_params=pltpu.CompilerParams(vmem_limit_bytes=8 * 1024 * 1024),
    )(up, lowg, cot_full)
    up = up.reshape(3, 3, 3, 16, 256).transpose(0, 1, 2, 4, 3)
    return up, lowg.reshape(3, 3, 3, 4, 256), cot_full.reshape(1, 2, 8, 8, 256)


def solution(mesh):
    placed = (
        P("sample", None, None, None, None),
        P("sample", None, None, None, "chan"),
        P(None, None, None, None, "chan"),
        P("sample", "chan", None, None, None),
    )
    return jax.shard_map(
        body,
        mesh=mesh,
        in_specs=placed,
        out_specs=(
            P(None, None, None, None, "chan"),
            P(None, None, None, "chan", None),
            P("sample", "chan", None, None, None),
        ),
        check_vma=False,
    )
```

```python
import jax
import jax.numpy as jnp
import numpy as np
from jax import lax
from jax.experimental import pallas as pl
from jax.experimental.pallas import tpu as pltpu
from jax.sharding import PartitionSpec as P

leak_slope = 0.3
BF = jnp.bfloat16
F32 = jnp.float32
NX, NZL, NC = 4, 3, 2
NZH, NY = 4, 8
NM = NX * NC
NZ = NZH * NZL
PIECE = 56


def tap_of(par, shift):
    if par == 0:
        return 1 if shift == 0 else None
    return 2 if shift == 0 else 0


def class_taps(p):
    found = []
    for q in range(8):
        taps = [tap_of((p >> b) & 1, (q >> b) & 1) for b in (2, 1, 0)]
        if None not in taps:
            found.append((q, taps[0] * 9 + taps[1] * 3 + taps[2]))
    return found


def tables():
    split = np.zeros((256, 256), np.float32)
    for p in range(8):
        pz, py, px = p >> 2, (p >> 1) & 1, p & 1
        for a in range(2):
            for b in range(4):
                for c in range(4):
                    split[p * 32 + a * 16 + b * 4 + c, (2 * a + pz) * 64 + (2 * b + py) * 8 + 2 * c + px] = 1
    merge = np.zeros((128, 128), np.float32)
    for p in range(8):
        pz, py, px = p >> 2, (p >> 1) & 1, p & 1
        for b in range(4):
            for c in range(4):
                merge[pz * 64 + (2 * b + py) * 8 + 2 * c + px, p * 16 + b * 4 + c] = 1
    spread16 = np.zeros((16, 128), np.float32)
    for q in range(8):
        for f in range(16):
            spread16[f, q * 16 + f] = 1
    shift = np.zeros((128, 512), np.float32)
    for k in range(4):
        dy, dx = k >> 1, k & 1
        for a in range(8):
            for b in range(4 - dy):
                for c in range(4 - dx):
                    shift[a * 16 + b * 4 + c, k * 128 + a * 16 + (b + dy) * 4 + c + dx] = 1
    order = np.zeros((128, 128), np.float32)
    for m in range(NM):
        for h in range(2):
            for y in range(8):
                order[m * 16 + h * 8 + y, 4 * ((2 * (m % 2) + h) * 8 + y) + m // 2] = 1
    pick = np.zeros((5, 512, 256), np.float32)
    for j in range(3):
        for k in range(3):
            for z in range(2):
                for y in range(8):
                    for x in range(8):
                        row, col = 2 * y + j - 1, 2 * x + k - 1
                        if row >= 0 and col >= 0:
                            pick[(j * 3 + k) // 2, z * 256 + row * 16 + col, (j * 3 + k) % 2 * 128 + z * 64 + y * 8 + x] = 1
    return split, merge, spread16, shift, order, pick, np.eye(256, dtype=np.float32), np.tile(spread16, (16, 1))


def mm(a, b):
    return jnp.dot(a, b, preferred_element_type=F32)


def kernel(
    act_hbm, cot_hbm, filt_hbm, low_hbm,
    split_hbm, merge_hbm, spread_hbm, shift_hbm, order_hbm, pick_hbm, eye_hbm, tall_hbm,
    out_up, out_low, out_cot,
    act_ref, cot_ref, fbuf, low_ref,
    split_ref, merge_ref, spread_ref, shift_ref, order_ref, pick_ref, eye_ref, tall_ref,
    wide_ref, wide_far, planes, qsend, qrecv, w_ref, wq_ref, a_ref, u_ref, urecv, uzl, ufin,
    r_ref, part, rlong, rshort,
    rim, t_ref, lstack, lsend, lrecv, call, res,
    dsend, drecv, ssum, zsend, zrecv, xrecv,
    load_sem, send_sem, recv_sem,
):
    s = lax.axis_index("sample")
    ch = lax.axis_index("chan")
    c = s % 2
    zl = (s // 2) % 3
    x = s // 6
    y = ch % 8
    zh = ch // 8
    m = x * 2 + c
    mate = (s + 1 - 2 * c, ch)

    def at_zh(d):
        return (s, jnp.bitwise_and(zh + d, NZH - 1) * 8 + y)

    def at_y(d):
        return (s, zh * 8 + jnp.bitwise_and(y + d, NY - 1))

    def m_at(r):
        return jnp.bitwise_and(m + r, NM - 1)

    def at_m(r):
        other = m_at(r)
        return (((other // 2) * 3 + zl) * 2 + other % 2, ch)

    def at_x(r):
        return ((jnp.bitwise_and(x + r, NX - 1) * 3 + zl) * 2 + c, ch)

    def from_x(r, core):
        return jnp.bitwise_and(x + NX - r, NX - 1) * 2 + core

    def at_z(zl_, zh_):
        return ((x * 3 + zl_) * 2 + c, zh_ * 8 + y)

    counter = [0]
    pending = []

    def remote(src, dst, dev):
        i = counter[0]
        counter[0] += 1
        cp = pltpu.make_async_remote_copy(
            src_ref=src, dst_ref=dst, send_sem=send_sem.at[i], recv_sem=recv_sem.at[i],
            device_id=dev, device_id_type=pl.DeviceIdType.MESH,
        )
        cp.start()
        pending.append(cp)
        return cp

    loads = {}
    for i, (name, src, dst) in enumerate((
        ("f0", filt_hbm.at[:, :, 0:128], fbuf.at[0, 0, 0:27]), ("f1", filt_hbm.at[:, :, 128:256], fbuf.at[0, 1, 0:27]),
        ("cot", cot_hbm, cot_ref), ("eye", eye_hbm, eye_ref), ("low", low_hbm, low_ref),
        ("spread", spread_hbm, spread_ref), ("shift", shift_hbm, shift_ref), ("tall", tall_hbm, tall_ref),
        ("split", split_hbm, split_ref), ("act", act_hbm, act_ref),
        ("order", order_hbm, order_ref), ("pick", pick_hbm, pick_ref), ("merge", merge_hbm, merge_ref),
    )):
        cp = pltpu.make_async_copy(src, dst, load_sem.at[i])
        cp.start()
        loads[name] = cp
    barrier = pltpu.get_barrier_semaphore()
    partners = []
    for dzh in (2, 1, 3, 0):
        for dzl in range(3):
            if dzl or dzh:
                partners.append(at_z(lax.rem(zl + dzl, 3), jnp.bitwise_and(zh + dzh, 3)))
    partners += [at_y(d) for d in (4, 3, 5, 2, 6, 1, 7)] + [at_m(r) for r in range(1, 8)]
    partners += [(s, lax.rem(ch + 1, 32)), (s, lax.rem(ch + 31, 32))]
    for dev in partners:
        pl.semaphore_signal(barrier, inc=1, device_id=dev, device_id_type=pl.DeviceIdType.MESH)

    fbuf[0, :, 27] = jnp.zeros((2, 16, 128), BF)

    for name in ("f0", "f1"):
        loads[name].wait()

    pl.semaphore_wait(barrier, len(partners))

    share = pl.ds(7 * x, 7)
    f_z = {}
    for d in (2, 1, 3):
        f_z[d] = remote(fbuf.at[0, c, share], fbuf.at[4 - d, c, share], at_zh(d))
    loads["low"].wait()
    rim_cp = remote(low_ref.at[3], rim, (s, lax.rem(ch + 1, 32)))
    loads["cot"].wait()
    loads["eye"].wait()
    planes[0:32, :] = lax.dot_general(
        cot_ref[...], eye_ref[...], (((0,), (0,)), ((), ())), preferred_element_type=F32
    )
    planes[32:40, :] = jnp.zeros((8, 256), F32)
    for q in range(4):
        qsend[q] = planes[8 * q : 8 * q + 16, :].astype(BF)
    q_cps = []
    for d in (2, 1, 3):
        q_cps.append(remote(qsend.at[jnp.bitwise_and(zh + d, NZH - 1)], qrecv.at[3 - d], at_zh(d)))

    lane = lax.broadcasted_iota(jnp.int32, (128, 128), 1) // 16

    def shifted(near, far):
        both = jnp.where(lane >= 4, far, near)
        terms = [jnp.where(lane % 4 == k, both, 0.0).astype(BF) for k in range(4)]
        return mm(shift_ref[...], jnp.concatenate(terms, axis=0)).astype(BF)

    loads["spread"].wait()
    loads["shift"].wait()
    for bc in range(16):
        got = lax.dot_general(
            cot_ref[bc * 16 : bc * 16 + 16, :], spread_ref[...], (((0,), (0,)), ((), ())), preferred_element_type=F32
        )
        wide_ref[pl.ds(bc, 32, stride=16), :] = got
    wide_ref[512:528, :] = jnp.zeros((16, 128), F32)
    for g in range(4):
        w_ref[g] = shifted(wide_ref[128 * g : 128 * g + 128, :], wide_ref[128 * g + 16 : 128 * g + 144, :])

    f_x = {}
    f_c = {}

    def spread_x(d):
        f_z[d].wait_recv()
        f_x[d] = [remote(fbuf.at[4 - d, c, share], fbuf.at[4 - d, c, share], at_x(r)) for r in (2, 1, 3)]

    def spread_c(d):
        for cp in f_x[d]:
            cp.wait_recv()
        f_c[d] = remote(fbuf.at[4 - d, c], fbuf.at[4 - d, c], mate)

    loads["order"].wait()
    loads["pick"].wait()
    rim_cp.wait_recv()
    edge = rim[...]
    edge = jnp.where(ch == 0, jnp.zeros_like(edge), edge)
    for q in range(5):
        plane = edge if q == 0 else low_ref[q - 1]
        got = lax.dot_general(order_ref[...], plane, (((1,), (1,)), ((), ())), preferred_element_type=F32)
        t_ref[q] = got.astype(BF)
    for i in range(3):
        lstack[i * 128 : i * 128 + 128, 0:256] = t_ref[i]
        lstack[i * 128 : i * 128 + 128, 256:512] = t_ref[i + 2]

    def window(jj, taps):
        got = mm(lstack[...], pick_ref[jj]).astype(BF)
        for i in range(3):
            for k in range(NM):
                for tap in taps:
                    rows = slice(i * 128 + k * 16, i * 128 + k * 16 + 16)
                    lsend[k, i * 9 + 2 * jj + tap] = got[rows, 128 * tap : 128 * tap + 128]

    def window_pair(jj, carry):
        window(jj, (0, 1))
        return carry

    lax.fori_loop(0, 2, window_pair, 0)
    spread_x(1)
    spread_x(3)
    lax.fori_loop(2, 4, window_pair, 0)
    window(4, (0,))
    spread_x(2)
    loads["tall"].wait()
    for cp in q_cps:
        cp.wait_recv()
    wq_ref[0] = w_ref[zh]
    group = lax.broadcasted_iota(jnp.int32, (48, 256), 1) // 16
    rows = jnp.concatenate([qrecv[0], qrecv[1], qrecv[2]], axis=0).astype(F32)
    for bc in range(16):
        got = mm(jnp.where(group == bc, rows, 0.0).astype(BF), tall_ref[...])
        for r in range(3):
            wide_far[r, pl.ds(bc, 16, stride=16), :] = got[r * 16 : r * 16 + 16]
    for r in range(3):
        wq_ref[r + 1] = shifted(wide_far[r, 0:128, :], wide_far[r, 16:144, :])
    spread_c(1)
    spread_c(3)
    spread_c(2)
    l_cps = []
    for r in range(1, NM):
        l_cps.append(remote(lsend.at[m_at(r)], lrecv.at[m], at_m(r)))

    left = jnp.concatenate([wq_ref[r] for r in range(4)], axis=1)
    for d in (1, 3, 2):
        f_c[d].wait_recv()

    def partial(p):
        taps = dict(class_taps(p))
        for r in range(4):
            for q in range(8):
                row = r * 128 + q * 16
                for half in range(2):
                    lanes = slice(128 * half, 128 * half + 128)
                    if q in taps:
                        r_ref[p % 2, row : row + 16, lanes] = fbuf[r, half, taps[q]]
                    else:
                        r_ref[p % 2, row : row + 16, lanes] = jnp.zeros((16, 128), BF)
        got = mm(left, r_ref[p % 2])
        for k in range(8):
            part[k, p] = got[k * 16 : k * 16 + 16]

    quarters = [pl.ds(2 * u, 2) for u in range(4)]
    way = (1, 7, 1, 7)
    back = (7, 1, 7, 1)
    longs = [[None] * 4 for _ in range(4)]
    shorts = [[None] * 4 for _ in range(3)]

    def ring(t, u):
        o = jnp.bitwise_and(y + way[u] * (4 - t), NY - 1)
        if t:
            longs[t - 1][u].wait_recv()
            part[o, quarters[u]] = part[o, quarters[u]] + rlong[t - 1, quarters[u]]
        longs[t][u] = remote(part.at[o, quarters[u]], rlong.at[t, quarters[u]], at_y(way[u]))
        if t < 3:
            o = jnp.bitwise_and(y + back[u] * (3 - t), NY - 1)
            if t:
                shorts[t - 1][u].wait_recv()
                part[o, quarters[u]] = part[o, quarters[u]] + rshort[t - 1, quarters[u]]
            shorts[t][u] = remote(part.at[o, quarters[u]], rshort.at[t, quarters[u]], at_y(back[u]))

    def split_group(g, carry):
        got = mm(split_ref[...], act_ref[pl.ds(pl.multiple_of(g * 256, 256), 256), :]).astype(BF)
        for p in range(8):
            a_ref[p, pl.ds(pl.multiple_of(g * 32, 32), 32), :] = got[p * 32 : p * 32 + 32]
        return carry

    def upper(p, wt):
        got = mm(wt, a_ref[p])
        for q, tap in class_taps(p):
            u_ref[tap * 16 : tap * 16 + 16, :] = got[q * 16 : q * 16 + 16]

    for u in range(4):
        partial(2 * u)
        partial(2 * u + 1)
        ring(0, u)
    loads["split"].wait()
    loads["act"].wait()
    lax.fori_loop(0, 6, split_group, 0)
    for u in range(4):
        ring(1, u)
        lax.fori_loop(6 + 3 * u, min(9 + 3 * u, 16), split_group, 0)
    for u in range(4):
        ring(2, u)
        if u == 0:
            wt = jnp.concatenate([jnp.transpose(w_ref[g].astype(F32)) for g in range(4)], axis=1).astype(BF)
        upper(2 * u, wt)
        upper(2 * u + 1, wt)
    u_ref[432:448, :] = jnp.zeros((16, 256), F32)
    u_cps = []
    for r in range(1, NM):
        u_cps.append(remote(u_ref.at[pl.ds(m_at(r) * PIECE, PIECE)], urecv.at[r - 1], at_m(r)))
    for u in range(4):
        ring(3, u)

    loads["merge"].wait()
    c_x = [[None] * 4 for _ in range(2)]
    c_m = [None] * 2
    for h in range(2):
        for u in (2 * h, 2 * h + 1):
            shorts[2][u].wait_recv()
            longs[3][u].wait_recv()
        both = pl.ds(4 * h, 4)
        total = part[y, both] + rlong[3, both] + rshort[2, both]
        total = total.reshape(64, 256)
        natural = jnp.dot(merge_ref[...], total, preferred_element_type=F32, precision=lax.Precision.HIGHEST)
        own = act_ref[pl.ds(pl.multiple_of(ch * 128 + h * 64, 64), 64), :].astype(F32)
        cot = natural * jnp.where(own > 0, 1.0, leak_slope)
        out_cot[h * 64 : h * 64 + 64, :] = cot
        call[m, h] = cot.astype(BF)
        for r in (2, 1, 3):
            c_x[h][r] = remote(call.at[m, h], call.at[m, h], at_x(r))
        c_m[h] = remote(call.at[m, h], call.at[m, h], mate)

    def terms(core):
        lhs = []
        rhs = []
        for r in range(NX):
            src = from_x(r, core)
            own = lsend[m] if r == 0 and core is c else lrecv[src]
            lhs.append(own.reshape(432, 128))
            rhs += [call[src, 0], call[src, 1]]
        return mm(jnp.concatenate(lhs, axis=1), jnp.concatenate(rhs, axis=0))

    for cp in l_cps:
        cp.wait_recv()
    c_f = [[None] * 4 for _ in range(2)]
    for h in range(2):
        for r in (1, 3, 2):
            c_x[h][r].wait_recv()
            got = from_x(r, c)
            c_f[h][r] = remote(call.at[got, h], call.at[got, h], mate)
    piece = u_ref[pl.ds(pl.multiple_of(m * PIECE, 8), PIECE), :]
    for r in range(1, NM):
        u_cps[r - 1].wait_recv()
        piece = piece + urecv[r - 1]
    uzl[zl] = piece
    uz_cps = []
    for d in (1, 2):
        uz_cps.append(remote(uzl.at[zl], uzl.at[zl], at_z(lax.rem(zl + d, 3), zh)))
    acc = terms(c)
    for h in range(2):
        c_m[h].wait_recv()
    for r in (1, 3, 2):
        for h in range(2):
            c_f[h][r].wait_recv()
    acc = acc + terms(1 - c)
    for half in range(2):
        res[half] = acc[:, 128 * half : 128 * half + 128]

    d_cps = [[None] * NY for _ in range(2)]
    for half in range(2):
        for k in range(NY):
            got = res[half, pl.ds(k, 54, stride=8), :].astype(BF)
            dsend[half, k] = jnp.concatenate([got, jnp.zeros((10, 128), BF)], axis=0)
        for r in (4, 3, 5, 2, 6, 1, 7):
            d_cps[half][r] = remote(dsend.at[half, jnp.bitwise_and(y + r, NY - 1)], drecv.at[half, r - 1], at_y(r))
    for cp in uz_cps:
        cp.wait_recv()
    ufin[m] = (uzl[0] + uzl[1] + uzl[2]) * (1.0 / 24.0)
    ug_cps = []
    for r in range(1, NM):
        ug_cps.append(remote(ufin.at[m], ufin.at[m], at_m(r)))

    myz = zh * 3 + zl
    home = zh // 2 == c
    zbase = counter[0]
    counter[0] += 2 * NZ
    zsends = []
    for half in range(2):
        total = res[half, pl.ds(y, 54, stride=8), :]
        for r in (1, 7, 2, 6, 3, 5, 4):
            d_cps[half][r].wait_recv()
            total = total + drecv[half, r - 1, 0:54].astype(F32)
        ssum[half] = total
        for h in range(2):
            got = ssum[half, pl.ds(h, 27, stride=2), :]
            zsend[half, h] = jnp.concatenate([got, jnp.zeros((5, 128), F32)], axis=0).astype(BF)
        for h in range(2):
            for l in range(3):
                tz = 2 * c + h
                i = counter[0]
                counter[0] += 1
                away = jnp.logical_or(tz != zh, zl != l)
                cp = pltpu.make_async_remote_copy(
                    src_ref=zsend.at[half, h], dst_ref=zrecv.at[half, myz], send_sem=send_sem.at[i],
                    recv_sem=recv_sem.at[zbase + half * NZ + myz], device_id=at_z(l, tz),
                    device_id_type=pl.DeviceIdType.MESH,
                )
                pl.when(away)(cp.start)
                zsends.append((away, cp))

    for cp in ug_cps:
        cp.wait_recv()
    for k in range(NM):
        rows = min(PIECE, 432 - k * PIECE)
        out_up[k * PIECE : k * PIECE + rows, :] = ufin[k, 0:rows]

    xbase = counter[0]
    counter[0] += 2 * NX
    xsends = []
    for half in range(2):

        @pl.when(home)
        def _():
            zrecv[half, myz] = zsend[half, zh - 2 * c]

        for j in range(NZ):
            cp = pltpu.make_async_remote_copy(
                src_ref=zsend.at[half, 0], dst_ref=zrecv.at[half, j], send_sem=send_sem.at[zbase + half * NZ + j],
                recv_sem=recv_sem.at[zbase + half * NZ + j], device_id=at_z(zl, zh),
                device_id_type=pl.DeviceIdType.MESH,
            )
            pl.when(jnp.logical_and(home, myz != j))(cp.wait_recv)

        @pl.when(home)
        def _():
            done = zrecv[half, 0].astype(F32)
            for j in range(1, NZ):
                done = done + zrecv[half, j].astype(F32)
            xrecv[half, x] = done * (1.0 / 24.0)

        for r in range(1, NM):
            i = counter[0]
            counter[0] += 1
            cp = pltpu.make_async_remote_copy(
                src_ref=xrecv.at[half, x], dst_ref=xrecv.at[half, x], send_sem=send_sem.at[i],
                recv_sem=recv_sem.at[xbase + half * NX + x], device_id=at_m(r),
                device_id_type=pl.DeviceIdType.MESH,
            )
            pl.when(home)(cp.start)
            xsends.append(cp)
    for half in range(2):
        for k in range(NX):
            cp = pltpu.make_async_remote_copy(
                src_ref=xrecv.at[half, k], dst_ref=xrecv.at[half, k], send_sem=send_sem.at[xbase + half * NX + k],
                recv_sem=recv_sem.at[xbase + half * NX + k], device_id=mate,
                device_id_type=pl.DeviceIdType.MESH,
            )
            pl.when(jnp.logical_not(jnp.logical_and(home, x == k)))(cp.wait_recv)
        for k in range(NX):
            out_low[:, k, 128 * half : 128 * half + 128] = xrecv[half, k, 0:27]

    for cp in pending:
        cp.wait_send()
    for away, cp in zsends:
        pl.when(away)(cp.wait_send)
    for cp in xsends:
        pl.when(home)(cp.wait_send)


def flush(a, b, c, out_a, out_b, out_c, sem):
    moves = [pltpu.make_async_copy(src, dst, sem.at[i]) for i, (src, dst) in enumerate(((a, out_a), (b, out_b), (c, out_c)))]
    for cp in moves:
        cp.start()
    for cp in moves:
        cp.wait()


def body(act_64, cot_32, filters_32, act_128):
    consts = [jnp.asarray(t, BF) for t in tables()]
    consts[1] = consts[1].astype(F32)[:64, :64]
    act = act_64.reshape(64 * 64, 256)
    cot = cot_32[0].transpose(1, 2, 3, 0).reshape(256, 32)
    filt = filters_32.transpose(0, 1, 2, 4, 3).reshape(27, 16, 256)
    low = act_128.reshape(4, 256, 128)
    operands = [pltpu.with_memory_space_constraint(t, pltpu.HBM) for t in (act, cot, filt, low, *consts)]
    vm = pltpu.VMEM
    up, lowg, cot_full = pl.pallas_call(
        kernel,
        out_shape=(
            jax.ShapeDtypeStruct((432, 256), F32),
            jax.ShapeDtypeStruct((27, 4, 256), F32),
            jax.ShapeDtypeStruct((128, 256), F32),
        ),
        in_specs=[pl.BlockSpec(memory_space=pltpu.HBM)] * len(operands),
        out_specs=[pl.BlockSpec(memory_space=pltpu.VMEM)] * 3,
        scratch_shapes=[
            vm(act.shape, BF), vm(cot.shape, BF), vm((4, 2, 28, 16, 128), BF), vm(low.shape, BF),
            *[vm(t.shape, t.dtype) for t in consts],
            vm((528, 128), F32), vm((3, 256, 128), F32), vm((40, 256), F32), vm((4, 16, 256), BF), vm((3, 16, 256), BF),
            vm((4, 128, 128), BF), vm((4, 128, 128), BF), vm((8, 512, 256), BF),
            vm((448, 256), F32), vm((7, PIECE, 256), F32), vm((3, PIECE, 256), F32), vm((NM, PIECE, 256), F32),
            vm((2, 512, 256), BF), vm((8, 8, 16, 256), F32), vm((4, 8, 16, 256), F32), vm((3, 8, 16, 256), F32),
            vm((256, 128), BF), vm((5, 128, 256), BF), vm((384, 512), BF),
            vm((NM, 27, 16, 128), BF), vm((NM, 27, 16, 128), BF),
            vm((NM, 2, 64, 256), BF), vm((2, 432, 128), F32),
            vm((2, 8, 64, 128), BF), vm((2, 7, 64, 128), BF), vm((2, 54, 128), F32),
            vm((2, 2, 32, 128), BF), vm((2, NZ, 32, 128), BF), vm((2, NX, 32, 128), F32),
            pltpu.SemaphoreType.DMA((16,)), pltpu.SemaphoreType.DMA((192,)), pltpu.SemaphoreType.DMA((192,)),
        ],
        compiler_params=pltpu.CompilerParams(
            collective_id=0, has_side_effects=True, vmem_limit_bytes=48 * 1024 * 1024
        ),
    )(*operands)
    up, lowg, cot_full = pl.pallas_call(
        flush,
        out_shape=tuple(jax.ShapeDtypeStruct(t.shape, t.dtype) for t in (up, lowg, cot_full)),
        in_specs=[pl.BlockSpec(memory_space=pltpu.VMEM)] * 3,
        out_specs=[pl.BlockSpec(memory_space=pltpu.HBM)] * 3,
        scratch_shapes=[pltpu.SemaphoreType.DMA((3,))],
        compiler_params=pltpu.CompilerParams(vmem_limit_bytes=8 * 1024 * 1024),
    )(up, lowg, cot_full)
    up = up.reshape(3, 3, 3, 16, 256).transpose(0, 1, 2, 4, 3)
    return up, lowg.reshape(3, 3, 3, 4, 256), cot_full.reshape(1, 2, 8, 8, 256)


def solution(mesh):
    placed = (
        P("sample", None, None, None, None),
        P("sample", None, None, None, "chan"),
        P(None, None, None, None, "chan"),
        P("sample", "chan", None, None, None),
    )
    return jax.shard_map(
        body,
        mesh=mesh,
        in_specs=placed,
        out_specs=(
            P(None, None, None, None, "chan"),
            P(None, None, None, "chan", None),
            P("sample", "chan", None, None, None),
        ),
        check_vma=False,
    )
```

```python
import jax
import jax.numpy as jnp
import numpy as np
from jax import lax
from jax.experimental import pallas as pl
from jax.experimental.pallas import tpu as pltpu
from jax.sharding import PartitionSpec as P

leak_slope = 0.3
BF = jnp.bfloat16
F32 = jnp.float32
NX, NZL, NC = 4, 3, 2
NZH, NY = 4, 8
NM = NX * NC
NZ = NZH * NZL
PIECE = 56


def tap_of(par, shift):
    if par == 0:
        return 1 if shift == 0 else None
    return 2 if shift == 0 else 0


def class_taps(p):
    found = []
    for q in range(8):
        taps = [tap_of((p >> b) & 1, (q >> b) & 1) for b in (2, 1, 0)]
        if None not in taps:
            found.append((q, taps[0] * 9 + taps[1] * 3 + taps[2]))
    return found


def tables():
    split = np.zeros((256, 256), np.float32)
    for p in range(8):
        pz, py, px = p >> 2, (p >> 1) & 1, p & 1
        for a in range(2):
            for b in range(4):
                for c in range(4):
                    split[p * 32 + a * 16 + b * 4 + c, (2 * a + pz) * 64 + (2 * b + py) * 8 + 2 * c + px] = 1
    merge = np.zeros((128, 128), np.float32)
    for p in range(8):
        pz, py, px = p >> 2, (p >> 1) & 1, p & 1
        for b in range(4):
            for c in range(4):
                merge[pz * 64 + (2 * b + py) * 8 + 2 * c + px, p * 16 + b * 4 + c] = 1
    spread16 = np.zeros((16, 128), np.float32)
    for q in range(8):
        for f in range(16):
            spread16[f, q * 16 + f] = 1
    shift = np.zeros((128, 512), np.float32)
    for k in range(4):
        dy, dx = k >> 1, k & 1
        for a in range(8):
            for b in range(4 - dy):
                for c in range(4 - dx):
                    shift[a * 16 + b * 4 + c, k * 128 + a * 16 + (b + dy) * 4 + c + dx] = 1
    order = np.zeros((128, 128), np.float32)
    for m in range(NM):
        for h in range(2):
            for y in range(8):
                order[m * 16 + h * 8 + y, 4 * ((2 * (m % 2) + h) * 8 + y) + m // 2] = 1
    pick = np.zeros((5, 512, 256), np.float32)
    for j in range(3):
        for k in range(3):
            for z in range(2):
                for y in range(8):
                    for x in range(8):
                        row, col = 2 * y + j - 1, 2 * x + k - 1
                        if row >= 0 and col >= 0:
                            pick[(j * 3 + k) // 2, z * 256 + row * 16 + col, (j * 3 + k) % 2 * 128 + z * 64 + y * 8 + x] = 1
    return split, merge, spread16, shift, order, pick, np.eye(256, dtype=np.float32), np.tile(spread16, (16, 1))


def mm(a, b):
    return jnp.dot(a, b, preferred_element_type=F32)


def kernel(
    act_hbm, cot_hbm, filt_hbm, low_hbm,
    split_hbm, merge_hbm, spread_hbm, shift_hbm, order_hbm, pick_hbm, eye_hbm, tall_hbm,
    out_up, out_low, out_cot,
    act_ref, cot_ref, fbuf, low_ref,
    split_ref, merge_ref, spread_ref, shift_ref, order_ref, pick_ref, eye_ref, tall_ref,
    wide_ref, wide_far, planes, qsend, qrecv, w_ref, wq_ref, a_ref, u_ref, urecv, uzl, ufin,
    r_ref, part, rlong, rshort,
    rim, t_ref, lstack, lsend, lrecv, call, res,
    dsend, drecv, ssum, zsend, zrecv, xrecv,
    load_sem, send_sem, recv_sem,
):
    s = lax.axis_index("sample")
    ch = lax.axis_index("chan")
    c = s % 2
    zl = (s // 2) % 3
    x = s // 6
    y = ch % 8
    zh = ch // 8
    m = x * 2 + c
    mate = (s + 1 - 2 * c, ch)

    def at_zh(d):
        return (s, jnp.bitwise_and(zh + d, NZH - 1) * 8 + y)

    def at_y(d):
        return (s, zh * 8 + jnp.bitwise_and(y + d, NY - 1))

    def m_at(r):
        return jnp.bitwise_and(m + r, NM - 1)

    def at_m(r):
        other = m_at(r)
        return (((other // 2) * 3 + zl) * 2 + other % 2, ch)

    def at_x(r):
        return ((jnp.bitwise_and(x + r, NX - 1) * 3 + zl) * 2 + c, ch)

    def from_x(r, core):
        return jnp.bitwise_and(x + NX - r, NX - 1) * 2 + core

    def at_z(zl_, zh_):
        return ((x * 3 + zl_) * 2 + c, zh_ * 8 + y)

    counter = [0]
    pending = []

    def remote(src, dst, dev):
        i = counter[0]
        counter[0] += 1
        cp = pltpu.make_async_remote_copy(
            src_ref=src, dst_ref=dst, send_sem=send_sem.at[i], recv_sem=recv_sem.at[i],
            device_id=dev, device_id_type=pl.DeviceIdType.MESH,
        )
        cp.start()
        pending.append(cp)
        return cp

    loads = {}
    for i, (name, src, dst) in enumerate((
        ("f0", filt_hbm.at[:, :, 0:128], fbuf.at[0, 0, 0:27]), ("f1", filt_hbm.at[:, :, 128:256], fbuf.at[0, 1, 0:27]),
        ("cot", cot_hbm, cot_ref), ("eye", eye_hbm, eye_ref), ("low", low_hbm, low_ref),
        ("spread", spread_hbm, spread_ref), ("shift", shift_hbm, shift_ref), ("tall", tall_hbm, tall_ref),
        ("split", split_hbm, split_ref), ("act", act_hbm, act_ref),
        ("order", order_hbm, order_ref), ("pick", pick_hbm, pick_ref), ("merge", merge_hbm, merge_ref),
    )):
        cp = pltpu.make_async_copy(src, dst, load_sem.at[i])
        cp.start()
        loads[name] = cp
    barrier = pltpu.get_barrier_semaphore()
    partners = []
    for dzh in (2, 1, 3, 0):
        for dzl in range(3):
            if dzl or dzh:
                partners.append(at_z(lax.rem(zl + dzl, 3), jnp.bitwise_and(zh + dzh, 3)))
    partners += [at_y(d) for d in (4, 3, 5, 2, 6, 1, 7)] + [at_m(r) for r in range(1, 8)]
    partners += [(s, lax.rem(ch + 1, 32)), (s, lax.rem(ch + 31, 32))]
    for dev in partners:
        pl.semaphore_signal(barrier, inc=1, device_id=dev, device_id_type=pl.DeviceIdType.MESH)

    fbuf[0, :, 27] = jnp.zeros((2, 16, 128), BF)

    loads["cot"].wait()
    loads["eye"].wait()
    planes[0:32, :] = lax.dot_general(
        cot_ref[...], eye_ref[...], (((0,), (0,)), ((), ())), preferred_element_type=F32
    )
    planes[32:40, :] = jnp.zeros((8, 256), F32)
    for q in range(4):
        qsend[q] = planes[8 * q : 8 * q + 16, :].astype(BF)
    for name in ("f0", "f1"):
        loads[name].wait()

    pl.semaphore_wait(barrier, len(partners))

    share = pl.ds(7 * x, 7)
    f_z = {}
    for d in (2, 1, 3):
        f_z[d] = remote(fbuf.at[0, c, share], fbuf.at[4 - d, c, share], at_zh(d))
    loads["low"].wait()
    rim_cp = remote(low_ref.at[3], rim, (s, lax.rem(ch + 1, 32)))
    q_cps = []
    for d in (2, 1, 3):
        q_cps.append(remote(qsend.at[jnp.bitwise_and(zh + d, NZH - 1)], qrecv.at[3 - d], at_zh(d)))

    lane = lax.broadcasted_iota(jnp.int32, (128, 128), 1) // 16

    def shifted(near, far):
        both = jnp.where(lane >= 4, far, near)
        terms = [jnp.where(lane % 4 == k, both, 0.0).astype(BF) for k in range(4)]
        return mm(shift_ref[...], jnp.concatenate(terms, axis=0)).astype(BF)

    f_x = {}
    f_c = {}

    def spread_x(d):
        f_z[d].wait_recv()
        f_x[d] = [remote(fbuf.at[4 - d, c, share], fbuf.at[4 - d, c, share], at_x(r)) for r in (2, 1, 3)]

    def spread_c(d):
        for cp in f_x[d]:
            cp.wait_recv()
        f_c[d] = remote(fbuf.at[4 - d, c], fbuf.at[4 - d, c], mate)

    loads["order"].wait()
    loads["pick"].wait()
    rim_cp.wait_recv()
    edge = rim[...]
    edge = jnp.where(ch == 0, jnp.zeros_like(edge), edge)
    for q in range(5):
        plane = edge if q == 0 else low_ref[q - 1]
        got = lax.dot_general(order_ref[...], plane, (((1,), (1,)), ((), ())), preferred_element_type=F32)
        t_ref[q] = got.astype(BF)
    for i in range(3):
        lstack[i * 128 : i * 128 + 128, 0:256] = t_ref[i]
        lstack[i * 128 : i * 128 + 128, 256:512] = t_ref[i + 2]

    def window(jj, taps):
        got = mm(lstack[...], pick_ref[jj]).astype(BF)
        for i in range(3):
            for k in range(NM):
                for tap in taps:
                    rows = slice(i * 128 + k * 16, i * 128 + k * 16 + 16)
                    lsend[k, i * 9 + 2 * jj + tap] = got[rows, 128 * tap : 128 * tap + 128]

    def window_pair(jj, carry):
        window(jj, (0, 1))
        return carry

    loads["split"].wait()
    loads["act"].wait()

    def split_group(g, carry):
        got = mm(split_ref[...], act_ref[pl.ds(pl.multiple_of(g * 256, 256), 256), :]).astype(BF)
        for p in range(8):
            a_ref[p, pl.ds(pl.multiple_of(g * 32, 32), 32), :] = got[p * 32 : p * 32 + 32]
        return carry

    lax.fori_loop(0, 2, window_pair, 0)
    spread_x(1)
    spread_x(3)
    lax.fori_loop(2, 4, window_pair, 0)
    window(4, (0,))
    spread_x(2)
    loads["tall"].wait()
    loads["shift"].wait()
    for cp in q_cps:
        cp.wait_recv()
    group = lax.broadcasted_iota(jnp.int32, (64, 256), 1) // 16
    rows = jnp.concatenate([qsend[zh], qrecv[0], qrecv[1], qrecv[2]], axis=0).astype(F32)
    for bc in range(16):
        got = mm(jnp.where(group == bc, rows, 0.0).astype(BF), tall_ref[...])
        for r in range(4):
            wide_far[r, pl.ds(bc, 16, stride=16), :] = got[r * 16 : r * 16 + 16]
    for r in range(4):
        wq_ref[r] = shifted(wide_far[r, 0:128, :], wide_far[r, 16:144, :])
    lax.fori_loop(0, 6, split_group, 0)
    spread_c(1)
    spread_c(3)
    lax.fori_loop(6, 10, split_group, 0)
    spread_c(2)
    l_cps = []
    for r in range(1, NM):
        l_cps.append(remote(lsend.at[m_at(r)], lrecv.at[m], at_m(r)))

    lax.fori_loop(10, 16, split_group, 0)
    left = jnp.concatenate([wq_ref[r] for r in range(4)], axis=1)
    for d in (1, 3, 2):
        f_c[d].wait_recv()

    def partial(p):
        taps = dict(class_taps(p))
        for r in range(4):
            for q in range(8):
                row = r * 128 + q * 16
                for half in range(2):
                    lanes = slice(128 * half, 128 * half + 128)
                    if q in taps:
                        r_ref[p % 2, row : row + 16, lanes] = fbuf[r, half, taps[q]]
                    else:
                        r_ref[p % 2, row : row + 16, lanes] = jnp.zeros((16, 128), BF)
        got = mm(left, r_ref[p % 2])
        for k in range(8):
            part[k, p] = got[k * 16 : k * 16 + 16]

    quarters = [pl.ds(2 * u, 2) for u in range(4)]
    way = (1, 7, 1, 7)
    back = (7, 1, 7, 1)
    longs = [[None] * 4 for _ in range(4)]
    shorts = [[None] * 4 for _ in range(3)]

    def ring(t, u):
        o = jnp.bitwise_and(y + way[u] * (4 - t), NY - 1)
        if t:
            longs[t - 1][u].wait_recv()
            part[o, quarters[u]] = part[o, quarters[u]] + rlong[t - 1, quarters[u]]
        longs[t][u] = remote(part.at[o, quarters[u]], rlong.at[t, quarters[u]], at_y(way[u]))
        if t < 3:
            o = jnp.bitwise_and(y + back[u] * (3 - t), NY - 1)
            if t:
                shorts[t - 1][u].wait_recv()
                part[o, quarters[u]] = part[o, quarters[u]] + rshort[t - 1, quarters[u]]
            shorts[t][u] = remote(part.at[o, quarters[u]], rshort.at[t, quarters[u]], at_y(back[u]))

    def upper(p, wt):
        got = mm(wt, a_ref[p])
        for q, tap in class_taps(p):
            u_ref[tap * 16 : tap * 16 + 16, :] = got[q * 16 : q * 16 + 16]

    for u in range(4):
        partial(2 * u)
        partial(2 * u + 1)
        ring(0, u)
    loads["spread"].wait()
    for u in range(4):
        ring(1, u)
        if u == 0:
            for bc in range(16):
                got = lax.dot_general(
                    cot_ref[bc * 16 : bc * 16 + 16, :], spread_ref[...], (((0,), (0,)), ((), ())),
                    preferred_element_type=F32,
                )
                wide_ref[pl.ds(bc, 32, stride=16), :] = got
            wide_ref[512:528, :] = jnp.zeros((16, 128), F32)
        if u == 1:
            for g in range(4):
                w_ref[g] = shifted(wide_ref[128 * g : 128 * g + 128, :], wide_ref[128 * g + 16 : 128 * g + 144, :])
            wt = jnp.concatenate([jnp.transpose(w_ref[g].astype(F32)) for g in range(4)], axis=1).astype(BF)
        if u > 1:
            for p in range(4 * u - 8, 4 * u - 4):
                upper(p, wt)
    u_ref[432:448, :] = jnp.zeros((16, 256), F32)
    u_cps = []
    for r in range(1, NM):
        u_cps.append(remote(u_ref.at[pl.ds(m_at(r) * PIECE, PIECE)], urecv.at[r - 1], at_m(r)))
    for u in range(4):
        ring(2, u)
    for u in range(4):
        ring(3, u)

    loads["merge"].wait()
    c_x = [[None] * 4 for _ in range(2)]
    c_m = [None] * 2
    for h in range(2):
        for u in (2 * h, 2 * h + 1):
            shorts[2][u].wait_recv()
            longs[3][u].wait_recv()
        both = pl.ds(4 * h, 4)
        total = part[y, both] + rlong[3, both] + rshort[2, both]
        total = total.reshape(64, 256)
        natural = jnp.dot(merge_ref[...], total, preferred_element_type=F32, precision=lax.Precision.HIGHEST)
        own = act_ref[pl.ds(pl.multiple_of(ch * 128 + h * 64, 64), 64), :].astype(F32)
        cot = natural * jnp.where(own > 0, 1.0, leak_slope)
        out_cot[h * 64 : h * 64 + 64, :] = cot
        call[m, h] = cot.astype(BF)
        for r in (2, 1, 3):
            c_x[h][r] = remote(call.at[m, h], call.at[m, h], at_x(r))
        c_m[h] = remote(call.at[m, h], call.at[m, h], mate)

    def terms(core):
        lhs = []
        rhs = []
        for r in range(NX):
            src = from_x(r, core)
            own = lsend[m] if r == 0 and core is c else lrecv[src]
            lhs.append(own.reshape(432, 128))
            rhs += [call[src, 0], call[src, 1]]
        return mm(jnp.concatenate(lhs, axis=1), jnp.concatenate(rhs, axis=0))

    for cp in l_cps:
        cp.wait_recv()
    c_f = [[None] * 4 for _ in range(2)]
    for h in range(2):
        for r in (1, 3, 2):
            c_x[h][r].wait_recv()
            got = from_x(r, c)
            c_f[h][r] = remote(call.at[got, h], call.at[got, h], mate)
    acc = terms(c)
    for h in range(2):
        c_m[h].wait_recv()
    for r in (1, 3, 2):
        for h in range(2):
            c_f[h][r].wait_recv()
    acc = acc + terms(1 - c)
    for half in range(2):
        res[half] = acc[:, 128 * half : 128 * half + 128]

    d_cps = [[None] * NY for _ in range(2)]
    for half in range(2):
        for k in range(NY):
            got = res[half, pl.ds(k, 54, stride=8), :].astype(BF)
            dsend[half, k] = jnp.concatenate([got, jnp.zeros((10, 128), BF)], axis=0)
        for r in (4, 3, 5, 2, 6, 1, 7):
            d_cps[half][r] = remote(dsend.at[half, jnp.bitwise_and(y + r, NY - 1)], drecv.at[half, r - 1], at_y(r))
    piece = u_ref[pl.ds(pl.multiple_of(m * PIECE, 8), PIECE), :]
    for r in range(1, NM):
        u_cps[r - 1].wait_recv()
        piece = piece + urecv[r - 1]
    uzl[zl] = piece
    uz_cps = []
    for d in (1, 2):
        uz_cps.append(remote(uzl.at[zl], uzl.at[zl], at_z(lax.rem(zl + d, 3), zh)))
    myz = zh * 3 + zl
    home = zh // 2 == c
    zbase = counter[0]
    counter[0] += 2 * NZ
    zsends = []
    for half in range(2):
        total = res[half, pl.ds(y, 54, stride=8), :]
        for r in (1, 7, 2, 6, 3, 5, 4):
            d_cps[half][r].wait_recv()
            total = total + drecv[half, r - 1, 0:54].astype(F32)
        ssum[half] = total
        for h in range(2):
            got = ssum[half, pl.ds(h, 27, stride=2), :]
            zsend[half, h] = jnp.concatenate([got, jnp.zeros((5, 128), F32)], axis=0).astype(BF)
        for h in range(2):
            for l in range(3):
                tz = 2 * c + h
                i = counter[0]
                counter[0] += 1
                away = jnp.logical_or(tz != zh, zl != l)
                cp = pltpu.make_async_remote_copy(
                    src_ref=zsend.at[half, h], dst_ref=zrecv.at[half, myz], send_sem=send_sem.at[i],
                    recv_sem=recv_sem.at[zbase + half * NZ + myz], device_id=at_z(l, tz),
                    device_id_type=pl.DeviceIdType.MESH,
                )
                pl.when(away)(cp.start)
                zsends.append((away, cp))

    for cp in uz_cps:
        cp.wait_recv()
    ufin[m] = (uzl[0] + uzl[1] + uzl[2]) * (1.0 / 24.0)
    ug_cps = []
    for r in range(1, NM):
        ug_cps.append(remote(ufin.at[m], ufin.at[m], at_m(r)))

    xbase = counter[0]
    counter[0] += 2 * NX
    xsends = []
    for half in range(2):

        @pl.when(home)
        def _():
            zrecv[half, myz] = zsend[half, zh - 2 * c]

        for j in range(NZ):
            cp = pltpu.make_async_remote_copy(
                src_ref=zsend.at[half, 0], dst_ref=zrecv.at[half, j], send_sem=send_sem.at[zbase + half * NZ + j],
                recv_sem=recv_sem.at[zbase + half * NZ + j], device_id=at_z(zl, zh),
                device_id_type=pl.DeviceIdType.MESH,
            )
            pl.when(jnp.logical_and(home, myz != j))(cp.wait_recv)

        @pl.when(home)
        def _():
            done = zrecv[half, 0].astype(F32)
            for j in range(1, NZ):
                done = done + zrecv[half, j].astype(F32)
            xrecv[half, x] = done * (1.0 / 24.0)

        for r in range(1, NM):
            i = counter[0]
            counter[0] += 1
            cp = pltpu.make_async_remote_copy(
                src_ref=xrecv.at[half, x], dst_ref=xrecv.at[half, x], send_sem=send_sem.at[i],
                recv_sem=recv_sem.at[xbase + half * NX + x], device_id=at_m(r),
                device_id_type=pl.DeviceIdType.MESH,
            )
            pl.when(home)(cp.start)
            xsends.append(cp)
    for cp in ug_cps:
        cp.wait_recv()
    for k in range(NM):
        rows = min(PIECE, 432 - k * PIECE)
        out_up[k * PIECE : k * PIECE + rows, :] = ufin[k, 0:rows]
    for half in range(2):
        for k in range(NX):
            cp = pltpu.make_async_remote_copy(
                src_ref=xrecv.at[half, k], dst_ref=xrecv.at[half, k], send_sem=send_sem.at[xbase + half * NX + k],
                recv_sem=recv_sem.at[xbase + half * NX + k], device_id=mate,
                device_id_type=pl.DeviceIdType.MESH,
            )
            pl.when(jnp.logical_not(jnp.logical_and(home, x == k)))(cp.wait_recv)
        for k in range(NX):
            out_low[:, k, 128 * half : 128 * half + 128] = xrecv[half, k, 0:27]

    for cp in pending:
        cp.wait_send()
    for away, cp in zsends:
        pl.when(away)(cp.wait_send)
    for cp in xsends:
        pl.when(home)(cp.wait_send)


def flush(a, b, c, out_a, out_b, out_c, sem):
    moves = [pltpu.make_async_copy(src, dst, sem.at[i]) for i, (src, dst) in enumerate(((a, out_a), (b, out_b), (c, out_c)))]
    for cp in moves:
        cp.start()
    for cp in moves:
        cp.wait()


def body(act_64, cot_32, filters_32, act_128):
    consts = [jnp.asarray(t, BF) for t in tables()]
    consts[1] = consts[1].astype(F32)[:64, :64]
    act = act_64.reshape(64 * 64, 256)
    cot = cot_32[0].transpose(1, 2, 3, 0).reshape(256, 32)
    filt = filters_32.transpose(0, 1, 2, 4, 3).reshape(27, 16, 256)
    low = act_128.reshape(4, 256, 128)
    operands = [pltpu.with_memory_space_constraint(t, pltpu.HBM) for t in (act, cot, filt, low, *consts)]
    vm = pltpu.VMEM
    up, lowg, cot_full = pl.pallas_call(
        kernel,
        out_shape=(
            jax.ShapeDtypeStruct((432, 256), F32),
            jax.ShapeDtypeStruct((27, 4, 256), F32),
            jax.ShapeDtypeStruct((128, 256), F32),
        ),
        in_specs=[pl.BlockSpec(memory_space=pltpu.HBM)] * len(operands),
        out_specs=[pl.BlockSpec(memory_space=pltpu.VMEM)] * 3,
        scratch_shapes=[
            vm(act.shape, BF), vm(cot.shape, BF), vm((4, 2, 28, 16, 128), BF), vm(low.shape, BF),
            *[vm(t.shape, t.dtype) for t in consts],
            vm((528, 128), F32), vm((4, 256, 128), F32), vm((40, 256), F32), vm((4, 16, 256), BF), vm((3, 16, 256), BF),
            vm((4, 128, 128), BF), vm((4, 128, 128), BF), vm((8, 512, 256), BF),
            vm((448, 256), F32), vm((7, PIECE, 256), F32), vm((3, PIECE, 256), F32), vm((NM, PIECE, 256), F32),
            vm((2, 512, 256), BF), vm((8, 8, 16, 256), F32), vm((4, 8, 16, 256), F32), vm((3, 8, 16, 256), F32),
            vm((256, 128), BF), vm((5, 128, 256), BF), vm((384, 512), BF),
            vm((NM, 27, 16, 128), BF), vm((NM, 27, 16, 128), BF),
            vm((NM, 2, 64, 256), BF), vm((2, 432, 128), F32),
            vm((2, 8, 64, 128), BF), vm((2, 7, 64, 128), BF), vm((2, 54, 128), F32),
            vm((2, 2, 32, 128), BF), vm((2, NZ, 32, 128), BF), vm((2, NX, 32, 128), F32),
            pltpu.SemaphoreType.DMA((16,)), pltpu.SemaphoreType.DMA((192,)), pltpu.SemaphoreType.DMA((192,)),
        ],
        compiler_params=pltpu.CompilerParams(
            collective_id=0, has_side_effects=True, vmem_limit_bytes=48 * 1024 * 1024
        ),
    )(*operands)
    up, lowg, cot_full = pl.pallas_call(
        flush,
        out_shape=tuple(jax.ShapeDtypeStruct(t.shape, t.dtype) for t in (up, lowg, cot_full)),
        in_specs=[pl.BlockSpec(memory_space=pltpu.VMEM)] * 3,
        out_specs=[pl.BlockSpec(memory_space=pltpu.HBM)] * 3,
        scratch_shapes=[pltpu.SemaphoreType.DMA((3,))],
        compiler_params=pltpu.CompilerParams(vmem_limit_bytes=8 * 1024 * 1024),
    )(up, lowg, cot_full)
    up = up.reshape(3, 3, 3, 16, 256).transpose(0, 1, 2, 4, 3)
    return up, lowg.reshape(3, 3, 3, 4, 256), cot_full.reshape(1, 2, 8, 8, 256)


def solution(mesh):
    placed = (
        P("sample", None, None, None, None),
        P("sample", None, None, None, "chan"),
        P(None, None, None, None, "chan"),
        P("sample", "chan", None, None, None),
    )
    return jax.shard_map(
        body,
        mesh=mesh,
        in_specs=placed,
        out_specs=(
            P(None, None, None, None, "chan"),
            P(None, None, None, "chan", None),
            P("sample", "chan", None, None, None),
        ),
        check_vma=False,
    )
```

```python
import jax
import jax.numpy as jnp
import numpy as np
from jax import lax
from jax.experimental import pallas as pl
from jax.experimental.pallas import tpu as pltpu
from jax.sharding import PartitionSpec as P

leak_slope = 0.3
BF = jnp.bfloat16
F32 = jnp.float32
NX, NZL, NC = 4, 3, 2
NZH, NY = 4, 8
NM = NX * NC
NZ = NZH * NZL
PIECE = 56


def tap_of(par, shift):
    if par == 0:
        return 1 if shift == 0 else None
    return 2 if shift == 0 else 0


def class_taps(p):
    found = []
    for q in range(8):
        taps = [tap_of((p >> b) & 1, (q >> b) & 1) for b in (2, 1, 0)]
        if None not in taps:
            found.append((q, taps[0] * 9 + taps[1] * 3 + taps[2]))
    return found


def tables():
    split = np.zeros((256, 256), np.float32)
    for p in range(8):
        pz, py, px = p >> 2, (p >> 1) & 1, p & 1
        for a in range(2):
            for b in range(4):
                for c in range(4):
                    split[p * 32 + a * 16 + b * 4 + c, (2 * a + pz) * 64 + (2 * b + py) * 8 + 2 * c + px] = 1
    merge = np.zeros((128, 128), np.float32)
    for p in range(8):
        pz, py, px = p >> 2, (p >> 1) & 1, p & 1
        for b in range(4):
            for c in range(4):
                merge[pz * 64 + (2 * b + py) * 8 + 2 * c + px, p * 16 + b * 4 + c] = 1
    spread16 = np.zeros((16, 128), np.float32)
    for q in range(8):
        for f in range(16):
            spread16[f, q * 16 + f] = 1
    shift = np.zeros((128, 512), np.float32)
    for k in range(4):
        dy, dx = k >> 1, k & 1
        for a in range(8):
            for b in range(4 - dy):
                for c in range(4 - dx):
                    shift[a * 16 + b * 4 + c, k * 128 + a * 16 + (b + dy) * 4 + c + dx] = 1
    order = np.zeros((128, 128), np.float32)
    for m in range(NM):
        for h in range(2):
            for y in range(8):
                order[m * 16 + h * 8 + y, 4 * ((2 * (m % 2) + h) * 8 + y) + m // 2] = 1
    pick = np.zeros((5, 512, 256), np.float32)
    for j in range(3):
        for k in range(3):
            for z in range(2):
                for y in range(8):
                    for x in range(8):
                        row, col = 2 * y + j - 1, 2 * x + k - 1
                        if row >= 0 and col >= 0:
                            pick[(j * 3 + k) // 2, z * 256 + row * 16 + col, (j * 3 + k) % 2 * 128 + z * 64 + y * 8 + x] = 1
    return split, merge, spread16, shift, order, pick, np.eye(256, dtype=np.float32), np.tile(spread16, (16, 1))


def mm(a, b):
    return jnp.dot(a, b, preferred_element_type=F32)


def kernel(
    act_hbm, cot_hbm, filt_hbm, low_hbm,
    split_hbm, merge_hbm, spread_hbm, shift_hbm, order_hbm, pick_hbm, eye_hbm, tall_hbm,
    out_up, out_low, out_cot,
    act_ref, cot_ref, fbuf, low_ref,
    split_ref, merge_ref, spread_ref, shift_ref, order_ref, pick_ref, eye_ref, tall_ref,
    wide_ref, wide_far, planes, qsend, qrecv, w_ref, wq_ref, a_ref, u_ref, urecv, uzl, ufin,
    r_ref, part, rlong, rshort,
    rim, t_ref, lstack, lsend, lrecv, call, res,
    dsend, drecv, ssum, zsend, zrecv, xrecv,
    load_sem, send_sem, recv_sem,
):
    s = lax.axis_index("sample")
    ch = lax.axis_index("chan")
    c = s % 2
    zl = (s // 2) % 3
    x = s // 6
    y = ch % 8
    zh = ch // 8
    m = x * 2 + c
    mate = (s + 1 - 2 * c, ch)

    def at_zh(d):
        return (s, jnp.bitwise_and(zh + d, NZH - 1) * 8 + y)

    def at_y(d):
        return (s, zh * 8 + jnp.bitwise_and(y + d, NY - 1))

    def m_at(r):
        return jnp.bitwise_and(m + r, NM - 1)

    def at_m(r):
        other = m_at(r)
        return (((other // 2) * 3 + zl) * 2 + other % 2, ch)

    def at_x(r):
        return ((jnp.bitwise_and(x + r, NX - 1) * 3 + zl) * 2 + c, ch)

    def from_x(r, core):
        return jnp.bitwise_and(x + NX - r, NX - 1) * 2 + core

    def at_z(zl_, zh_):
        return ((x * 3 + zl_) * 2 + c, zh_ * 8 + y)

    counter = [0]
    pending = []

    def remote(src, dst, dev):
        i = counter[0]
        counter[0] += 1
        cp = pltpu.make_async_remote_copy(
            src_ref=src, dst_ref=dst, send_sem=send_sem.at[i], recv_sem=recv_sem.at[i],
            device_id=dev, device_id_type=pl.DeviceIdType.MESH,
        )
        cp.start()
        pending.append(cp)
        return cp

    barrier = pltpu.get_barrier_semaphore()
    partners = [at_y(d) for d in range(1, 8)] + [at_m(r) for r in range(1, 8)]
    partners += [(s, lax.rem(ch + 1, 32)), (s, lax.rem(ch + 31, 32))]
    for dzl in range(3):
        for dzh in range(4):
            if dzl or dzh:
                partners.append(at_z(lax.rem(zl + dzl, 3), jnp.bitwise_and(zh + dzh, 3)))
    for dev in partners:
        pl.semaphore_signal(barrier, inc=1, device_id=dev, device_id_type=pl.DeviceIdType.MESH)

    loads = {}
    for i, (name, src, dst) in enumerate((
        ("f0", filt_hbm.at[:, :, 0:128], fbuf.at[0, 0, 0:27]), ("f1", filt_hbm.at[:, :, 128:256], fbuf.at[0, 1, 0:27]),
        ("cot", cot_hbm, cot_ref), ("eye", eye_hbm, eye_ref), ("low", low_hbm, low_ref),
        ("spread", spread_hbm, spread_ref), ("shift", shift_hbm, shift_ref), ("tall", tall_hbm, tall_ref),
        ("split", split_hbm, split_ref), ("act", act_hbm, act_ref),
        ("order", order_hbm, order_ref), ("pick", pick_hbm, pick_ref), ("merge", merge_hbm, merge_ref),
    )):
        cp = pltpu.make_async_copy(src, dst, load_sem.at[i])
        cp.start()
        loads[name] = cp
    fbuf[0, :, 27] = jnp.zeros((2, 16, 128), BF)

    loads["cot"].wait()
    loads["eye"].wait()
    planes[0:32, :] = lax.dot_general(
        cot_ref[...], eye_ref[...], (((0,), (0,)), ((), ())), preferred_element_type=F32
    )
    planes[32:40, :] = jnp.zeros((8, 256), F32)
    for q in range(4):
        qsend[q] = planes[8 * q : 8 * q + 16, :].astype(BF)
    for name in ("f0", "f1", "low"):
        loads[name].wait()

    pl.semaphore_wait(barrier, len(partners))

    share = pl.ds(7 * x, 7)
    f_z = {}
    for d in (2, 1, 3):
        f_z[d] = remote(fbuf.at[0, c, share], fbuf.at[4 - d, c, share], at_zh(d))
    q_cps = []
    for d in (2, 1, 3):
        q_cps.append(remote(qsend.at[jnp.bitwise_and(zh + d, NZH - 1)], qrecv.at[3 - d], at_zh(d)))
    rim_cp = remote(low_ref.at[3], rim, (s, lax.rem(ch + 1, 32)))

    lane = lax.broadcasted_iota(jnp.int32, (128, 128), 1) // 16

    def shifted(near, far):
        both = jnp.where(lane >= 4, far, near)
        terms = [jnp.where(lane % 4 == k, both, 0.0).astype(BF) for k in range(4)]
        return mm(shift_ref[...], jnp.concatenate(terms, axis=0)).astype(BF)

    loads["spread"].wait()
    loads["shift"].wait()
    for bc in range(16):
        got = lax.dot_general(
            cot_ref[bc * 16 : bc * 16 + 16, :], spread_ref[...], (((0,), (0,)), ((), ())), preferred_element_type=F32
        )
        wide_ref[pl.ds(bc, 32, stride=16), :] = got
    wide_ref[512:528, :] = jnp.zeros((16, 128), F32)
    for g in range(4):
        w_ref[g] = shifted(wide_ref[128 * g : 128 * g + 128, :], wide_ref[128 * g + 16 : 128 * g + 144, :])

    loads["split"].wait()
    loads["act"].wait()

    def split_group(g, carry):
        got = mm(split_ref[...], act_ref[pl.ds(pl.multiple_of(g * 256, 256), 256), :]).astype(BF)
        for p in range(8):
            a_ref[p, pl.ds(pl.multiple_of(g * 32, 32), 32), :] = got[p * 32 : p * 32 + 32]
        return carry

    lax.fori_loop(0, 16, split_group, 0)

    f_x = {}
    f_c = {}

    def spread_x(d):
        f_z[d].wait_recv()
        f_x[d] = [remote(fbuf.at[4 - d, c, share], fbuf.at[4 - d, c, share], at_x(r)) for r in (2, 1, 3)]

    def spread_c(d):
        for cp in f_x[d]:
            cp.wait_recv()
        f_c[d] = remote(fbuf.at[4 - d, c], fbuf.at[4 - d, c], mate)

    spread_x(1)
    spread_x(3)

    wt = jnp.concatenate([jnp.transpose(w_ref[g].astype(F32)) for g in range(4)], axis=1).astype(BF)
    for p in range(8):
        got = mm(wt, a_ref[p])
        for q, tap in class_taps(p):
            u_ref[tap * 16 : tap * 16 + 16, :] = got[q * 16 : q * 16 + 16]
    u_ref[432:448, :] = jnp.zeros((16, 256), F32)
    spread_x(2)
    loads["order"].wait()
    loads["pick"].wait()
    rim_cp.wait_recv()
    edge = rim[...]
    edge = jnp.where(ch == 0, jnp.zeros_like(edge), edge)
    for q in range(5):
        plane = edge if q == 0 else low_ref[q - 1]
        got = lax.dot_general(order_ref[...], plane, (((1,), (1,)), ((), ())), preferred_element_type=F32)
        t_ref[q] = got.astype(BF)
    for i in range(3):
        lstack[i * 128 : i * 128 + 128, 0:256] = t_ref[i]
        lstack[i * 128 : i * 128 + 128, 256:512] = t_ref[i + 2]
    loads["tall"].wait()
    for cp in q_cps:
        cp.wait_recv()
    wq_ref[0] = w_ref[zh]
    group = lax.broadcasted_iota(jnp.int32, (48, 256), 1) // 16
    rows = jnp.concatenate([qrecv[0], qrecv[1], qrecv[2]], axis=0).astype(F32)
    for bc in range(16):
        got = mm(jnp.where(group == bc, rows, 0.0).astype(BF), tall_ref[...])
        for r in range(3):
            wide_far[r, pl.ds(bc, 16, stride=16), :] = got[r * 16 : r * 16 + 16]
    for r in range(3):
        wq_ref[r + 1] = shifted(wide_far[r, 0:128, :], wide_far[r, 16:144, :])
    spread_c(1)
    spread_c(3)

    def window(jj, taps):
        got = mm(lstack[...], pick_ref[jj]).astype(BF)
        for i in range(3):
            for k in range(NM):
                for tap in taps:
                    rows = slice(i * 128 + k * 16, i * 128 + k * 16 + 16)
                    lsend[k, i * 9 + 2 * jj + tap] = got[rows, 128 * tap : 128 * tap + 128]

    def window_pair(jj, carry):
        window(jj, (0, 1))
        return carry

    lax.fori_loop(0, 2, window_pair, 0)
    spread_c(2)
    u_cps = []
    for r in range(1, NM):
        u_cps.append(remote(u_ref.at[pl.ds(m_at(r) * PIECE, PIECE)], urecv.at[r - 1], at_m(r)))

    lax.fori_loop(2, 4, window_pair, 0)
    window(4, (0,))
    l_cps = []
    for r in range(1, NM):
        l_cps.append(remote(lsend.at[m_at(r)], lrecv.at[m], at_m(r)))

    left = jnp.concatenate([wq_ref[r] for r in range(4)], axis=1)
    for d in (1, 3, 2):
        f_c[d].wait_recv()

    def partial(p):
        taps = dict(class_taps(p))
        for r in range(4):
            for q in range(8):
                row = r * 128 + q * 16
                for half in range(2):
                    lanes = slice(128 * half, 128 * half + 128)
                    if q in taps:
                        r_ref[p % 2, row : row + 16, lanes] = fbuf[r, half, taps[q]]
                    else:
                        r_ref[p % 2, row : row + 16, lanes] = jnp.zeros((16, 128), BF)
        got = mm(left, r_ref[p % 2])
        for k in range(8):
            part[k, p] = got[k * 16 : k * 16 + 16]

    quarters = [pl.ds(2 * u, 2) for u in range(4)]
    way = (1, 7, 1, 7)
    back = (7, 1, 7, 1)
    longs = [[None] * 4 for _ in range(4)]
    shorts = [[None] * 4 for _ in range(3)]

    def ring(t, u):
        o = jnp.bitwise_and(y + way[u] * (4 - t), NY - 1)
        if t:
            longs[t - 1][u].wait_recv()
            part[o, quarters[u]] = part[o, quarters[u]] + rlong[t - 1, quarters[u]]
        longs[t][u] = remote(part.at[o, quarters[u]], rlong.at[t, quarters[u]], at_y(way[u]))
        if t < 3:
            o = jnp.bitwise_and(y + back[u] * (3 - t), NY - 1)
            if t:
                shorts[t - 1][u].wait_recv()
                part[o, quarters[u]] = part[o, quarters[u]] + rshort[t - 1, quarters[u]]
            shorts[t][u] = remote(part.at[o, quarters[u]], rshort.at[t, quarters[u]], at_y(back[u]))

    for u in range(4):
        partial(2 * u)
        partial(2 * u + 1)
        ring(0, u)
    for t in (1, 2):
        for u in range(4):
            ring(t, u)
    piece = u_ref[pl.ds(pl.multiple_of(m * PIECE, 8), PIECE), :]
    for r in range(1, NM):
        u_cps[r - 1].wait_recv()
        piece = piece + urecv[r - 1]
    uzl[zl] = piece
    uz_cps = []
    for d in (1, 2):
        uz_cps.append(remote(uzl.at[zl], uzl.at[zl], at_z(lax.rem(zl + d, 3), zh)))
    for u in range(4):
        ring(3, u)

    loads["merge"].wait()
    c_x = [[None] * 4 for _ in range(2)]
    c_m = [None] * 2
    for h in range(2):
        for u in (2 * h, 2 * h + 1):
            shorts[2][u].wait_recv()
            longs[3][u].wait_recv()
        both = pl.ds(4 * h, 4)
        total = part[y, both] + rlong[3, both] + rshort[2, both]
        total = total.reshape(64, 256)
        natural = jnp.dot(merge_ref[...], total, preferred_element_type=F32, precision=lax.Precision.HIGHEST)
        own = act_ref[pl.ds(pl.multiple_of(ch * 128 + h * 64, 64), 64), :].astype(F32)
        cot = natural * jnp.where(own > 0, 1.0, leak_slope)
        out_cot[h * 64 : h * 64 + 64, :] = cot
        call[m, h] = cot.astype(BF)
        for r in (2, 1, 3):
            c_x[h][r] = remote(call.at[m, h], call.at[m, h], at_x(r))
        c_m[h] = remote(call.at[m, h], call.at[m, h], mate)

    def terms(core):
        lhs = []
        rhs = []
        for r in range(NX):
            src = from_x(r, core)
            own = lsend[m] if r == 0 and core is c else lrecv[src]
            lhs.append(own.reshape(432, 128))
            rhs += [call[src, 0], call[src, 1]]
        return mm(jnp.concatenate(lhs, axis=1), jnp.concatenate(rhs, axis=0))

    for cp in l_cps:
        cp.wait_recv()
    c_f = [[None] * 4 for _ in range(2)]
    for h in range(2):
        for r in (1, 3, 2):
            c_x[h][r].wait_recv()
            got = from_x(r, c)
            c_f[h][r] = remote(call.at[got, h], call.at[got, h], mate)
    for cp in uz_cps:
        cp.wait_recv()
    ufin[m] = (uzl[0] + uzl[1] + uzl[2]) * (1.0 / 24.0)
    acc = terms(c)
    for h in range(2):
        c_m[h].wait_recv()
    for r in (1, 3, 2):
        for h in range(2):
            c_f[h][r].wait_recv()
    acc = acc + terms(1 - c)
    for half in range(2):
        res[half] = acc[:, 128 * half : 128 * half + 128]

    d_cps = [[None] * NY for _ in range(2)]
    for half in range(2):
        for k in range(NY):
            got = res[half, pl.ds(k, 54, stride=8), :].astype(BF)
            dsend[half, k] = jnp.concatenate([got, jnp.zeros((10, 128), BF)], axis=0)
        for r in (4, 3, 5, 2, 6, 1, 7):
            d_cps[half][r] = remote(dsend.at[half, jnp.bitwise_and(y + r, NY - 1)], drecv.at[half, r - 1], at_y(r))
    ug_cps = []
    for r in range(1, NM):
        ug_cps.append(remote(ufin.at[m], ufin.at[m], at_m(r)))

    myz = zh * 3 + zl
    home = zh // 2 == c
    zbase = counter[0]
    counter[0] += 2 * NZ
    zsends = []
    for half in range(2):
        total = res[half, pl.ds(y, 54, stride=8), :]
        for r in (1, 7, 2, 6, 3, 5, 4):
            d_cps[half][r].wait_recv()
            total = total + drecv[half, r - 1, 0:54].astype(F32)
        ssum[half] = total
        for h in range(2):
            got = ssum[half, pl.ds(h, 27, stride=2), :]
            zsend[half, h] = jnp.concatenate([got, jnp.zeros((5, 128), F32)], axis=0).astype(BF)
        for h in range(2):
            for l in range(3):
                tz = 2 * c + h
                i = counter[0]
                counter[0] += 1
                away = jnp.logical_or(tz != zh, zl != l)
                cp = pltpu.make_async_remote_copy(
                    src_ref=zsend.at[half, h], dst_ref=zrecv.at[half, myz], send_sem=send_sem.at[i],
                    recv_sem=recv_sem.at[zbase + half * NZ + myz], device_id=at_z(l, tz),
                    device_id_type=pl.DeviceIdType.MESH,
                )
                pl.when(away)(cp.start)
                zsends.append((away, cp))

    for cp in ug_cps:
        cp.wait_recv()
    for k in range(NM):
        rows = min(PIECE, 432 - k * PIECE)
        out_up[k * PIECE : k * PIECE + rows, :] = ufin[k, 0:rows]

    xbase = counter[0]
    counter[0] += 2 * NX
    xsends = []
    for half in range(2):

        @pl.when(home)
        def _():
            zrecv[half, myz] = zsend[half, zh - 2 * c]

        for j in range(NZ):
            cp = pltpu.make_async_remote_copy(
                src_ref=zsend.at[half, 0], dst_ref=zrecv.at[half, j], send_sem=send_sem.at[zbase + half * NZ + j],
                recv_sem=recv_sem.at[zbase + half * NZ + j], device_id=at_z(zl, zh),
                device_id_type=pl.DeviceIdType.MESH,
            )
            pl.when(jnp.logical_and(home, myz != j))(cp.wait_recv)

        @pl.when(home)
        def _():
            done = zrecv[half, 0].astype(F32)
            for j in range(1, NZ):
                done = done + zrecv[half, j].astype(F32)
            xrecv[half, x] = done * (1.0 / 24.0)

        for r in range(1, NM):
            i = counter[0]
            counter[0] += 1
            cp = pltpu.make_async_remote_copy(
                src_ref=xrecv.at[half, x], dst_ref=xrecv.at[half, x], send_sem=send_sem.at[i],
                recv_sem=recv_sem.at[xbase + half * NX + x], device_id=at_m(r),
                device_id_type=pl.DeviceIdType.MESH,
            )
            pl.when(home)(cp.start)
            xsends.append(cp)
    for half in range(2):
        for k in range(NX):
            cp = pltpu.make_async_remote_copy(
                src_ref=xrecv.at[half, k], dst_ref=xrecv.at[half, k], send_sem=send_sem.at[xbase + half * NX + k],
                recv_sem=recv_sem.at[xbase + half * NX + k], device_id=mate,
                device_id_type=pl.DeviceIdType.MESH,
            )
            pl.when(jnp.logical_not(jnp.logical_and(home, x == k)))(cp.wait_recv)
        for k in range(NX):
            out_low[:, k, 128 * half : 128 * half + 128] = xrecv[half, k, 0:27]

    for cp in pending:
        cp.wait_send()
    for away, cp in zsends:
        pl.when(away)(cp.wait_send)
    for cp in xsends:
        pl.when(home)(cp.wait_send)


def flush(a, b, c, out_a, out_b, out_c, sem):
    moves = [pltpu.make_async_copy(src, dst, sem.at[i]) for i, (src, dst) in enumerate(((a, out_a), (b, out_b), (c, out_c)))]
    for cp in moves:
        cp.start()
    for cp in moves:
        cp.wait()


def body(act_64, cot_32, filters_32, act_128):
    consts = [jnp.asarray(t, BF) for t in tables()]
    consts[1] = consts[1].astype(F32)[:64, :64]
    act = act_64.reshape(64 * 64, 256)
    cot = cot_32[0].transpose(1, 2, 3, 0).reshape(256, 32)
    filt = filters_32.transpose(0, 1, 2, 4, 3).reshape(27, 16, 256)
    low = act_128.reshape(4, 256, 128)
    operands = [pltpu.with_memory_space_constraint(t, pltpu.HBM) for t in (act, cot, filt, low, *consts)]
    vm = pltpu.VMEM
    up, lowg, cot_full = pl.pallas_call(
        kernel,
        out_shape=(
            jax.ShapeDtypeStruct((432, 256), F32),
            jax.ShapeDtypeStruct((27, 4, 256), F32),
            jax.ShapeDtypeStruct((128, 256), F32),
        ),
        in_specs=[pl.BlockSpec(memory_space=pltpu.HBM)] * len(operands),
        out_specs=[pl.BlockSpec(memory_space=pltpu.VMEM)] * 3,
        scratch_shapes=[
            vm(act.shape, BF), vm(cot.shape, BF), vm((4, 2, 28, 16, 128), BF), vm(low.shape, BF),
            *[vm(t.shape, t.dtype) for t in consts],
            vm((528, 128), F32), vm((3, 256, 128), F32), vm((40, 256), F32), vm((4, 16, 256), BF), vm((3, 16, 256), BF),
            vm((4, 128, 128), BF), vm((4, 128, 128), BF), vm((8, 512, 256), BF),
            vm((448, 256), F32), vm((7, PIECE, 256), F32), vm((3, PIECE, 256), F32), vm((NM, PIECE, 256), F32),
            vm((2, 512, 256), BF), vm((8, 8, 16, 256), F32), vm((4, 8, 16, 256), F32), vm((3, 8, 16, 256), F32),
            vm((256, 128), BF), vm((5, 128, 256), BF), vm((384, 512), BF),
            vm((NM, 27, 16, 128), BF), vm((NM, 27, 16, 128), BF),
            vm((NM, 2, 64, 256), BF), vm((2, 432, 128), F32),
            vm((2, 8, 64, 128), BF), vm((2, 7, 64, 128), BF), vm((2, 54, 128), F32),
            vm((2, 2, 32, 128), BF), vm((2, NZ, 32, 128), BF), vm((2, NX, 32, 128), F32),
            pltpu.SemaphoreType.DMA((16,)), pltpu.SemaphoreType.DMA((192,)), pltpu.SemaphoreType.DMA((192,)),
        ],
        compiler_params=pltpu.CompilerParams(
            collective_id=0, has_side_effects=True, vmem_limit_bytes=48 * 1024 * 1024
        ),
    )(*operands)
    up, lowg, cot_full = pl.pallas_call(
        flush,
        out_shape=tuple(jax.ShapeDtypeStruct(t.shape, t.dtype) for t in (up, lowg, cot_full)),
        in_specs=[pl.BlockSpec(memory_space=pltpu.VMEM)] * 3,
        out_specs=[pl.BlockSpec(memory_space=pltpu.HBM)] * 3,
        scratch_shapes=[pltpu.SemaphoreType.DMA((3,))],
        compiler_params=pltpu.CompilerParams(vmem_limit_bytes=8 * 1024 * 1024),
    )(up, lowg, cot_full)
    up = up.reshape(3, 3, 3, 16, 256).transpose(0, 1, 2, 4, 3)
    return up, lowg.reshape(3, 3, 3, 4, 256), cot_full.reshape(1, 2, 8, 8, 256)


def solution(mesh):
    placed = (
        P("sample", None, None, None, None),
        P("sample", None, None, None, "chan"),
        P(None, None, None, None, "chan"),
        P("sample", "chan", None, None, None),
    )
    return jax.shard_map(
        body,
        mesh=mesh,
        in_specs=placed,
        out_specs=(
            P(None, None, None, None, "chan"),
            P(None, None, None, "chan", None),
            P("sample", "chan", None, None, None),
        ),
        check_vma=False,
    )
```
